512 devices in a mesh: head: 8 (over x, core), seq: 64 (over z, y).
Axes of the slice: x: 4, y: 8, z: 8, core: 2. Of those that a mesh axis runs over, the one named last changes fastest.
Arguments:
- query_rows: bfloat16 [8, 32768, 512], P('head', 'seq'), may hold values from -16 to 16
- key_rows: bfloat16 [8, 32768, 512], P('head', 'seq'), may hold values from -16 to 16
- value_rows: bfloat16 [8, 32768, 512], P('head', 'seq'), may hold values from -6 to 6
- step_rate: float32 [8, 32768], P('head', 'seq'), may hold values from 0.15 to 162
- doc_start: int32 [32768], P('seq'), may hold values from 0 to 32767, as said below
- speech_flag: int32 [32768], P('seq'), may hold values 0 or 1
- w_gate: bfloat16 [8, 512, 512], P('head'), may hold values from -0.25 to 0.25
- w_up: bfloat16 [8, 512, 512], P('head'), may hold values from -0.25 to 0.25
- w_down: bfloat16 [8, 512, 512], P('head'), may hold values from -0.25 to 0.25
- w_cond: bfloat16 [4096, 512], P('head'), may hold values from -0.09375 to 0.09375
Outputs:
- mixed: bfloat16 [8, 32768, 512], P('head', 'seq')
- cond: bfloat16 [64, 512, 512], P('seq', 'head')
The draws below stay inside these ranges and needn't reach their ends.
Inputs may be any that keep to these rules, and one draw needn't show every extreme that they name: doc_start[p] is the position of the first token of the document holding token p: at most p, never falling along the sequence, and doc_start[q] = q wherever a document begins; the last token begins a document of its own.
All inputs are finite; a program needn't handle non-finite values. No bound on the sum of `speech_flag` on one device may be relied on, other than what follows from the above.
Results may differ from the reference program's by a relative error of at most 0.015.
Values may be sent and summed in bfloat16 or wider, within the bound.
No kernel may reach another device: no remote copies, remote signals or barrier semaphores. Data moves between devices by JAX's collectives and lax.ppermute only.
A program may use at most 64 MiB of HBM per device.

```python
import math
import jax
import jax.numpy as jnp
from jax import lax

HEADS = 8
HD = 512
COND = 512
WIN = 512
TOK_DEV = 512
TOKENS = 32768
UPDATE_TOK = 16384
WIDTH = 4096
N_SEQ = 64


def query_key_pair(key):
    base_key = jax.random.fold_in(key, 7)
    keys_all = jax.random.split(base_key, 2)
    query_base = jnp.clip(jax.random.normal(keys_all[0], (HEADS, TOKENS, HD), jnp.float32), -6.0, 6.0)
    key_base = jnp.clip(jax.random.normal(keys_all[1], (HEADS, TOKENS, HD), jnp.float32), -6.0, 6.0)
    return (query_base, key_base)


def draw_query_rows(key, part):
    return query_key_pair(key)[0].astype(jnp.bfloat16)


def draw_key_rows(key, part):
    return query_key_pair(key)[1].astype(jnp.bfloat16)


def draw_step_rate(key, part):
    keys_all = jax.random.split(jax.random.fold_in(key, 11), 2)
    position = jnp.arange(TOKENS, dtype=jnp.float32) / TOKENS
    head_scale = jnp.exp(jax.random.uniform(keys_all[1], (HEADS, 1), jnp.float32, math.log(0.5), math.log(2.0)))
    ramp = jnp.exp(math.log(9.0) * position)
    jitter = jnp.exp(jax.random.uniform(keys_all[0], (HEADS, TOKENS), jnp.float32, math.log(0.3), math.log(3.0)))
    return (jitter * ramp[None, :] * head_scale).astype(jnp.float32)


def draw_doc_start(key, part):
    marks = jax.random.randint(jax.random.fold_in(key, 23), (TOKENS,), 0, 2 * WIN)
    position = jnp.arange(TOKENS, dtype=jnp.int32)
    begins = jnp.where((marks == 0) | (position == 0) | (position == TOKENS - 1), position, 0)
    return lax.cummax(begins, axis=0).astype(jnp.int32)


def place_ends(entries, key, smallest, largest):
    index_at = [jax.random.randint(jax.random.fold_in(key, axis), (), 0, length) for axis, length in enumerate(entries.shape)]
    main_axis = entries.shape.index(max(entries.shape))
    beside = index_at[:main_axis] + [(index_at[main_axis] + 1) % entries.shape[main_axis]] + index_at[main_axis + 1:]
    return entries.at[tuple(index_at)].set(smallest).at[tuple(beside)].set(largest)


def block_levels(own_key, shape, cuts, least, high):
    loudness, own = 1.0, jax.random.fold_in(own_key, 6)
    for dim, shards_of in cuts:
        draws = jnp.exp(jax.random.uniform(jax.random.fold_in(own, dim), (shards_of,), jnp.float32, least / len(cuts), high / len(cuts)))
        loudness = loudness * jnp.repeat(draws, shape[dim] // shards_of).reshape([-1 if axis == dim else 1 for axis in range(len(shape))])
    return loudness


def scatter_about(key, dims, spread, most, cuts=(), kind=jnp.bfloat16):
    entries = spread * jax.random.normal(key, dims, jnp.float32)
    if cuts:
        entries = entries * block_levels(key, dims, cuts, -0.22, 0.18)
    return jnp.clip(entries, -most, most).astype(kind)


def setup_inputs(seed: int = 0) -> dict:
    seeds = jax.random.split(jax.random.key(seed), 11)
    query_rows = draw_query_rows(jax.random.fold_in(seeds[10], 71), 0)
    key_rows = draw_key_rows(jax.random.fold_in(seeds[10], 71), 0)
    value_rows = scatter_about(seeds[2], (HEADS, TOKENS, HD), 1.0, 6.0, ((0, 8), (1, 64)))
    step_rate = draw_step_rate(jax.random.fold_in(seeds[10], 71), 0)
    doc_start = draw_doc_start(jax.random.fold_in(seeds[10], 71), 0)
    speech_flag = place_ends((jax.random.randint(seeds[5], (TOKENS,), 0, 2) < 1).astype(jnp.int32), jax.random.fold_in(seeds[5], 1), 0, 1)
    w_gate = scatter_about(seeds[6], (HEADS, HD, HD), HD ** -0.5, 0.25, ((0, 8),))
    w_up = scatter_about(seeds[7], (HEADS, HD, HD), HD ** -0.5, 0.25, ((0, 8),))
    w_down = scatter_about(seeds[8], (HEADS, HD, HD), HD ** -0.5, 0.25, ((0, 8),))
    w_cond = scatter_about(seeds[9], (WIDTH, COND), WIDTH ** -0.5, 0.09375, ((0, 8),))
    return {"query_rows": query_rows, "key_rows": key_rows, "value_rows": value_rows, "step_rate": step_rate, "doc_start": doc_start, "speech_flag": speech_flag, "w_gate": w_gate, "w_up": w_up, "w_down": w_down, "w_cond": w_cond}


eps_norm = 1e-06

def renormed(old_weight, summed, factor):
    old_f = old_weight.astype(jnp.float32)
    updated = old_f + summed * factor[:, None, None]
    old_norm = jnp.sqrt(lax.optimization_barrier(jnp.sum(old_f * old_f, axis=-1, keepdims=True)))
    new_norm = jnp.sqrt(lax.optimization_barrier(jnp.sum(updated * updated, axis=-1, keepdims=True)) + eps_norm)
    return (updated * (old_norm / new_norm)).astype(jnp.bfloat16)

def fast_apply(rows_in, weight_gate, weight_up, weight_down):
    gate_pre = jnp.einsum('htd,hrd->htr', rows_in.astype(jnp.float32), weight_gate.astype(jnp.float32))
    up_pre = jnp.einsum('htd,hrd->htr', rows_in.astype(jnp.float32), weight_up.astype(jnp.float32))
    hidden = (gate_pre * jax.nn.sigmoid(gate_pre) * up_pre).astype(jnp.bfloat16)
    return jnp.einsum('htr,hdr->htd', hidden.astype(jnp.float32), weight_down.astype(jnp.float32))

def reference(query_rows, key_rows, value_rows, step_rate, doc_start, speech_flag, w_gate, w_up, w_down, w_cond):
    block_rows = min(512, TOKENS)
    score_scale = 1.0 / math.sqrt(HD)

    def attend_head(operands):
        query_head, key_head, value_head = operands
        key_pad = jnp.concatenate([jnp.zeros((WIN, HD), key_head.dtype), key_head], axis=0)
        value_pad = jnp.concatenate([jnp.zeros((WIN, HD), value_head.dtype), value_head], axis=0)

        def one_block(row_start):
            query_blk = lax.dynamic_slice_in_dim(query_head, row_start, block_rows, 0)
            key_blk = lax.dynamic_slice_in_dim(key_pad, row_start, WIN + block_rows, 0)
            value_blk = lax.dynamic_slice_in_dim(value_pad, row_start, WIN + block_rows, 0)
            starts_doc = lax.dynamic_slice_in_dim(doc_start, row_start, block_rows, 0)
            pos_query = row_start + jnp.arange(block_rows, dtype=jnp.int32)
            pos_key = row_start - WIN + jnp.arange(WIN + block_rows, dtype=jnp.int32)
            allowed = (pos_key[None, :] <= pos_query[:, None]) & (pos_key[None, :] > pos_query[:, None] - WIN) & (pos_key[None, :] >= starts_doc[:, None])
            scores = jnp.dot(query_blk, key_blk.T, preferred_element_type=jnp.float32) * score_scale
            scores = jnp.where(allowed, scores, -1e+30)
            row_max = lax.optimization_barrier(jnp.max(scores, axis=-1, keepdims=True))
            expon = jnp.exp(scores - row_max)
            prob_bf = (expon / lax.optimization_barrier(jnp.sum(expon, axis=-1, keepdims=True))).astype(jnp.bfloat16)
            return jnp.dot(prob_bf, value_blk, preferred_element_type=jnp.float32)
        starts = jnp.arange(TOKENS // block_rows, dtype=jnp.int32) * block_rows
        return lax.map(one_block, starts).reshape(TOKENS, HD)
    attended = lax.map(attend_head, (query_rows, key_rows, value_rows))
    speech_on = speech_flag.astype(jnp.float32)
    key_first = key_rows[:, :UPDATE_TOK]
    scaled = (speech_on[None, :UPDATE_TOK, None] * step_rate[:, :UPDATE_TOK, None] * value_rows[:, :UPDATE_TOK].astype(jnp.float32)).astype(jnp.bfloat16)
    gate_pre = jnp.einsum('htd,hrd->htr', key_first.astype(jnp.float32), w_gate.astype(jnp.float32))
    up_pre = jnp.einsum('htd,hrd->htr', key_first.astype(jnp.float32), w_up.astype(jnp.float32))
    sigma = jax.nn.sigmoid(gate_pre)
    active = gate_pre * sigma
    hidden_zero = (active * up_pre).astype(jnp.bfloat16)
    back = jnp.einsum('htd,hdr->htr', scaled.astype(jnp.float32), w_down.astype(jnp.float32))
    grad_gate = (back * up_pre * sigma * (1.0 + gate_pre * (1.0 - sigma))).astype(jnp.bfloat16)
    grad_up = (back * active).astype(jnp.bfloat16)
    sum_gate = jnp.einsum('htr,htd->hrd', grad_gate.astype(jnp.float32), key_first.astype(jnp.float32))
    sum_up = jnp.einsum('htr,htd->hrd', grad_up.astype(jnp.float32), key_first.astype(jnp.float32))
    sum_down = jnp.einsum('htd,htr->hdr', scaled.astype(jnp.float32), hidden_zero.astype(jnp.float32))
    totals = lax.optimization_barrier(jnp.sum(step_rate[:, :UPDATE_TOK], axis=1))
    factor = 2.0 * UPDATE_TOK / (totals * math.sqrt(UPDATE_TOK * HD))
    new_gate = renormed(w_gate, sum_gate, factor)
    new_up = renormed(w_up, sum_up, factor)
    new_down = renormed(w_down, sum_down, factor)
    fast_first = fast_apply(query_rows[:, :UPDATE_TOK], w_gate, w_up, w_down)
    fast_second = fast_apply(query_rows[:, UPDATE_TOK:], new_gate, new_up, new_down)
    fast_out = jnp.concatenate([fast_first, fast_second], axis=1)
    mixed = (attended + fast_out).astype(jnp.bfloat16)
    cond_weight = w_cond.reshape(HEADS, HD, COND).astype(jnp.float32)
    projected = jnp.einsum('htd,hdc->tc', mixed.astype(jnp.float32), cond_weight)
    cond = (projected * speech_on[:, None]).astype(jnp.bfloat16).reshape(N_SEQ, TOK_DEV, COND)
    return (mixed, cond)
```

```python
import functools
import math
import jax
import jax.numpy as jnp
from jax import lax
from jax.experimental import pallas as pl
from jax.experimental.pallas import tpu as pltpu
from jax.sharding import PartitionSpec as P

F32 = jnp.float32
BF16 = jnp.bfloat16
NN = (((1,), (0,)), ((), ()))
NT = (((1,), (1,)), ((), ()))


def dot(a, b, dims):
    return lax.dot_general(a, b, dims, preferred_element_type=F32)


def grads_kernel(k_ref, v_ref, rate_ref, flag_ref, wg_ref, wu_ref, wd_ref, out_ref):
    key = k_ref[0]
    rate = rate_ref[...]
    coeff = flag_ref[...].astype(F32) * rate
    scaled = (coeff * v_ref[0].T.astype(F32)).astype(BF16)
    down = wd_ref[0].T
    step = 128
    part = step // 16

    def put(piece, which, start):
        for c in range(4):
            block = piece[:, c * 128 : (c + 1) * 128].reshape(part, 16, 128)
            row = which * 64 + c * 16
            out_ref[start // 16 : start // 16 + part, row : row + 16, :] = block

    hidden = []
    for start in range(0, 512, step):
        rows = slice(start, start + step)
        gate = dot(wg_ref[0, rows, :], key, NT)
        up = dot(wu_ref[0, rows, :], key, NT)
        back = dot(down[rows], scaled, NN)
        sigma = jax.nn.sigmoid(gate)
        active = gate * sigma
        hidden.append((active * up).astype(BF16))
        grad_gate = (back * up * sigma * (1.0 + gate * (1.0 - sigma))).astype(BF16)
        grad_up = (back * active).astype(BF16)
        put(dot(grad_gate, key, NN).astype(BF16), 0, start)
        put(dot(grad_up, key, NN).astype(BF16), 1, start)
    hidden = jnp.concatenate(hidden, axis=0)
    for start in range(0, 512, step):
        rows = slice(start, start + step)
        put(dot(scaled[rows], hidden, NT).astype(BF16), 2, start)
    total = jnp.sum(rate, axis=1, keepdims=True)
    high = total.astype(BF16)
    low = (total - high.astype(F32)).astype(BF16)
    row = lax.broadcasted_iota(jnp.int32, (8, 128), 0)
    tail = jnp.where(row == 0, high.astype(F32), jnp.where(row == 1, low.astype(F32), 0.0))
    out_ref[:, 192:200, :] = jnp.broadcast_to(tail.astype(BF16)[None], (32, 8, 128))


def grads(k, v, rate, flag, wg, wu, wd):
    return pl.pallas_call(
        grads_kernel,
        out_shape=jax.ShapeDtypeStruct((32, 200, 128), BF16),
        in_specs=[pl.BlockSpec(memory_space=pltpu.VMEM)] * 7,
        out_specs=pl.BlockSpec(memory_space=pltpu.VMEM),
        name="grads",
    )(k, v, rate, flag, wg, wu, wd)


def renorm_kernel(rank_ref, recv_ref, wg_ref, wu_ref, wd_ref, out_ref, *, update_len):
    head = recv_ref[:, 192:200, :].astype(F32)
    tail = jnp.sum(head, axis=0)
    total = tail[0:1, 0:1] + tail[1:2, 0:1]
    factor = 2.0 * update_len / (total * math.sqrt(update_len * 512))
    for which, ref in enumerate((wg_ref, wu_ref, wd_ref)):
        old = ref[0].astype(F32)
        pieces = []
        for c in range(4):
            row = which * 64 + c * 16
            pieces.append(jnp.sum(recv_ref[:, row : row + 16, :].astype(F32), axis=0))
        summed = jnp.concatenate(pieces, axis=1)
        updated = old + summed * factor
        old_norm = jnp.sqrt(jnp.sum(old * old, axis=-1, keepdims=True))
        new_norm = jnp.sqrt(jnp.sum(updated * updated, axis=-1, keepdims=True) + 1e-6)
        out_ref[which] = (updated * (old_norm / new_norm)).astype(BF16)


def renorm(rank, recv, wg, wu, wd, update_len):
    wspec = pl.BlockSpec((1, 16, 512), lambda i, r: (0, r[0], 0))
    return pl.pallas_call(
        functools.partial(renorm_kernel, update_len=update_len),
        out_shape=jax.ShapeDtypeStruct((3, 16, 512), BF16),
        grid_spec=pltpu.PrefetchScalarGridSpec(
            num_scalar_prefetch=1,
            grid=(1,),
            in_specs=[pl.BlockSpec((32, 200, 128), lambda i, r: (0, 0, 0)), wspec, wspec, wspec],
            out_specs=pl.BlockSpec((3, 16, 512), lambda i, r: (0, 0, 0)),
        ),
        name="renorm",
    )(rank, recv, wg, wu, wd)


def attend_kernel(pos_ref, q_ref, pk_ref, k_ref, pv_ref, v_ref, doc_ref, out_ref):
    base = pos_ref[0]
    step = 128
    scale = 1.0 / math.sqrt(512)
    doc = (jnp.broadcast_to(doc_ref[...], (8, 512)) - base).T[:, :1]
    for start in range(0, 512, step):
        rows = slice(start, start + step)
        q = q_ref[0, rows, :]
        keys = jnp.concatenate([pk_ref[0, start:, :], k_ref[0, : start + step, :]], axis=0)
        vals = jnp.concatenate([pv_ref[0, start:, :], v_ref[0, : start + step, :]], axis=0)
        width = 512 + step
        s = dot(q, keys, NT) * scale
        at = lax.broadcasted_iota(jnp.int32, (step, width), 0) + start
        to = lax.broadcasted_iota(jnp.int32, (step, width), 1) + (start - 512)
        ok = (to <= at) & (to > at - 512) & (to >= doc[rows])
        s = jnp.where(ok, s, -1e30)
        top = jnp.max(s, axis=-1, keepdims=True)
        e = jnp.exp(s - top)
        prob = (e / jnp.sum(e, axis=-1, keepdims=True)).astype(BF16)
        out_ref[rows, :] = dot(prob, vals, NN)


def attend(pos, q, pk, k, pv, v, doc):
    vm = pl.BlockSpec(memory_space=pltpu.VMEM)
    return pl.pallas_call(
        attend_kernel,
        out_shape=jax.ShapeDtypeStruct((512, 512), F32),
        in_specs=[pl.BlockSpec(memory_space=pltpu.SMEM)] + [vm] * 6,
        out_specs=vm,
        name="attend",
    )(pos, q, pk, k, pv, v, doc)


def apply_kernel(first_ref, q_ref, att_ref, wg0, wu0, wd0, fresh, wc_ref, mixed_ref, part_ref, w, sem):
    first = first_ref[0] == 1

    @pl.when(first)
    def _():
        for i, ref in enumerate((wg0, wu0, wd0)):
            pltpu.make_async_copy(ref, w.at[i], sem.at[i]).start()

    @pl.when(jnp.logical_not(first))
    def _():
        for i in range(3):
            pltpu.make_async_copy(fresh.at[:, i], w.at[i], sem.at[i]).start()

    for i in range(3):
        pltpu.make_async_copy(fresh.at[:, i], w.at[i], sem.at[i]).wait()
    step = 128
    for start in range(0, 512, step):
        rows = slice(start, start + step)
        q = q_ref[0, rows, :]
        gate = dot(q, w[0].reshape(512, 512), NT)
        up = dot(q, w[1].reshape(512, 512), NT)
        hidden = (gate * jax.nn.sigmoid(gate) * up).astype(BF16)
        mixed = (att_ref[rows, :] + dot(hidden, w[2].reshape(512, 512), NT)).astype(BF16)
        mixed_ref[0, rows, :] = mixed
        part_ref[rows, :] = dot(mixed, wc_ref[...], NN).astype(BF16)


def fast_apply(first, q, att, wg, wu, wd, fresh, wc):
    vm = pl.BlockSpec(memory_space=pltpu.VMEM)
    hb = pl.BlockSpec(memory_space=pl.ANY)
    return pl.pallas_call(
        apply_kernel,
        out_shape=(
            jax.ShapeDtypeStruct((1, 512, 512), BF16),
            jax.ShapeDtypeStruct((512, 512), BF16),
        ),
        in_specs=[pl.BlockSpec(memory_space=pltpu.SMEM), vm, vm, hb, hb, hb, hb, vm],
        out_specs=(vm, vm),
        scratch_shapes=[pltpu.VMEM((3, 32, 16, 512), BF16), pltpu.SemaphoreType.DMA((3,))],
        name="fast_apply",
    )(first, q, att, *(x.reshape(32, 16, 512) for x in (wg, wu, wd)), fresh, wc)


def combine_kernel(recv_ref, flag_ref, out_ref):
    summed = jnp.sum(recv_ref[...].astype(F32), axis=0)
    flag = jnp.broadcast_to(flag_ref[...].astype(F32), (8, 64)).T[:, :1]
    out_ref[0] = (summed * flag).astype(BF16)


def combine(recv, flag):
    vm = pl.BlockSpec(memory_space=pltpu.VMEM)
    return pl.pallas_call(
        combine_kernel,
        out_shape=jax.ShapeDtypeStruct((1, 64, 512), BF16),
        in_specs=[vm, vm],
        out_specs=vm,
        name="combine",
    )(recv, flag)


def local(q, k, v, rate, doc_start, flag, wg, wu, wd, wc):
    seq_count = lax.axis_size("seq")
    half = seq_count // 2
    index = lax.axis_index("seq")
    first = index < half
    rank = lax.rem(index, half)
    halves = [list(range(half)), list(range(half, seq_count))]
    route = [(i - 1, i) for i in range(1, seq_count)]
    pk = lax.ppermute(k, "seq", route)
    pv = lax.ppermute(v, "seq", route)
    terms = grads(k, v, rate, flag[None], wg, wu, wd)
    recv = lax.all_to_all(terms, "seq", 0, 0, axis_index_groups=halves)
    shard = renorm(rank[None].astype(jnp.int32), recv, wg, wu, wd, 512 * half)
    shard = lax.ppermute(shard, "seq", [(i, i + half) for i in range(half)])
    fresh = lax.all_gather(shard, "seq", axis=0, axis_index_groups=halves)
    att = attend((index * 512)[None].astype(jnp.int32), q, pk, k, pv, v, doc_start[None])
    mixed, part = fast_apply(first[None].astype(jnp.int32), q, att, wg, wu, wd, fresh, wc)
    got = lax.all_to_all(part.reshape(8, 64, 512), "head", 0, 0)
    flags = lax.dynamic_slice_in_dim(flag, lax.axis_index("head") * 64, 64, 0)
    return mixed, combine(got, flags[None])


def solution(mesh):
    placed = (
        P("head", "seq", None),
        P("head", "seq", None),
        P("head", "seq", None),
        P("head", "seq"),
        P("seq"),
        P("seq"),
        P("head", None, None),
        P("head", None, None),
        P("head", None, None),
        P("head", None),
    )
    return jax.shard_map(
        local,
        mesh=mesh,
        in_specs=placed,
        out_specs=(P("head", "seq", None), P("seq", "head", None)),
        check_vma=False,
    )
```

```python
import functools
import math
import jax
import jax.numpy as jnp
from jax import lax
from jax.experimental import pallas as pl
from jax.experimental.pallas import tpu as pltpu
from jax.sharding import PartitionSpec as P


F32 = jnp.float32
GRADS_STEP = 256
APPLY_STEP = 256
BF16 = jnp.bfloat16
NN = (((1,), (0,)), ((), ()))
NT = (((1,), (1,)), ((), ()))


def dot(a, b, dims):
    return lax.dot_general(a, b, dims, preferred_element_type=F32)


def grads_kernel(
    k_hbm, v_hbm, wg_hbm, wu_hbm, wd_hbm, rate_ref, flag_ref, out_hbm,
    k_s, v_s, wg_s, wu_s, wd_s, out_s, sem_in, sem_out,
):
    loads = [
        pltpu.make_async_copy(src.at[0], dst, sem_in.at[i])
        for i, (src, dst) in enumerate(
            ((v_hbm, v_s), (wd_hbm, wd_s), (k_hbm, k_s), (wg_hbm, wg_s), (wu_hbm, wu_s))
        )
    ]
    for load in loads:
        load.start()
    step = GRADS_STEP
    part = step // 16
    stores = []

    def put(piece, which, start):
        for c in range(4):
            block = piece[:, c * 128 : (c + 1) * 128].reshape(part, 16, 128)
            row = which * 64 + c * 16
            out_s[start // 16 : start // 16 + part, row : row + 16, :] = block

    def ship(low, high, start, rows):
        window = (slice(start // 16, (start + rows) // 16), slice(low, high))
        store = pltpu.make_async_copy(out_s.at[window], out_hbm.at[window], sem_out.at[len(stores)])
        store.start()
        stores.append(store)

    rate = rate_ref[...]
    coeff = flag_ref[...].astype(F32) * rate
    total = jnp.sum(rate, axis=1, keepdims=True)
    high = total.astype(BF16)
    low = (total - high.astype(F32)).astype(BF16)
    row = lax.broadcasted_iota(jnp.int32, (8, 128), 0)
    tail = jnp.where(row == 0, high.astype(F32), jnp.where(row == 1, low.astype(F32), 0.0))
    out_s[:, 192:200, :] = jnp.broadcast_to(tail.astype(BF16)[None], (32, 8, 128))
    loads[0].wait()
    scaled = (coeff * v_s[...].T.astype(F32)).astype(BF16)
    loads[1].wait()
    down = wd_s[...].T
    for load in loads[2:]:
        load.wait()
    key = k_s[...]
    hidden = []
    for start in range(0, 512, step):
        rows = slice(start, start + step)
        gate = dot(wg_s[rows, :], key, NT)
        up = dot(wu_s[rows, :], key, NT)
        back = dot(down[rows], scaled, NN)
        sigma = jax.nn.sigmoid(gate)
        active = gate * sigma
        hidden.append((active * up).astype(BF16))
        grad_gate = (back * up * sigma * (1.0 + gate * (1.0 - sigma))).astype(BF16)
        grad_up = (back * active).astype(BF16)
        put(dot(grad_gate, key, NN).astype(BF16), 0, start)
        put(dot(grad_up, key, NN).astype(BF16), 1, start)
        ship(0, 128, start, step)
    hidden = jnp.concatenate(hidden, axis=0)
    for start in range(0, 512, step):
        rows = slice(start, start + step)
        put(dot(scaled[rows], hidden, NT).astype(BF16), 2, start)
        ship(128, 200, start, step)
    for store in stores:
        store.wait()


def grads(k, v, rate, flag, wg, wu, wd):
    vm = pl.BlockSpec(memory_space=pltpu.VMEM)
    hb = pl.BlockSpec(memory_space=pltpu.HBM)
    return pl.pallas_call(
        grads_kernel,
        out_shape=jax.ShapeDtypeStruct((32, 200, 128), BF16),
        in_specs=[hb] * 5 + [vm, vm],
        out_specs=hb,
        scratch_shapes=[pltpu.VMEM((512, 512), BF16)] * 5
        + [
            pltpu.VMEM((32, 200, 128), BF16),
            pltpu.SemaphoreType.DMA((5,)),
            pltpu.SemaphoreType.DMA((2 * (512 // GRADS_STEP),)),
        ],
        name="grads",
    )(k, v, wg, wu, wd, rate, flag)


def renorm_kernel(
    rank_ref, recv_ref, wg, wu, wd, out, old_s, new_s, sem_in, sem_out, *, update_len
):
    rows = pl.ds(pl.multiple_of(rank_ref[0] * 16, 16), 16)
    loads = [
        pltpu.make_async_copy(ref.at[0, rows], old_s.at[i], sem_in.at[i])
        for i, ref in enumerate((wg, wu, wd))
    ]
    for load in loads:
        load.start()
    tail = jnp.sum(recv_ref[:, 192:200, :].astype(F32), axis=0)
    total = tail[0:1, 0:1] + tail[1:2, 0:1]
    factor = 2.0 * update_len / (total * math.sqrt(update_len * 512))
    for which in range(3):
        pieces = []
        for c in range(4):
            row = which * 64 + c * 16
            pieces.append(jnp.sum(recv_ref[:, row : row + 16, :].astype(F32), axis=0))
        summed = jnp.concatenate(pieces, axis=1)
        loads[which].wait()
        old = old_s[which].astype(F32)
        updated = old + summed * factor
        old_norm = jnp.sqrt(jnp.sum(old * old, axis=-1, keepdims=True))
        new_norm = jnp.sqrt(jnp.sum(updated * updated, axis=-1, keepdims=True) + 1e-6)
        new_s[which] = (updated * (old_norm / new_norm)).astype(BF16)
    stores = [pltpu.make_async_copy(new_s, out.at[d], sem_out.at[d]) for d in range(8)]
    for store in stores:
        store.start()
    for store in stores:
        store.wait()


def renorm(rank, recv, wg, wu, wd, update_len):
    hb = pl.BlockSpec(memory_space=pltpu.HBM)
    return pl.pallas_call(
        functools.partial(renorm_kernel, update_len=update_len),
        out_shape=jax.ShapeDtypeStruct((8, 3, 16, 512), BF16),
        in_specs=[
            pl.BlockSpec(memory_space=pltpu.SMEM),
            pl.BlockSpec(memory_space=pltpu.VMEM),
            hb,
            hb,
            hb,
        ],
        out_specs=hb,
        scratch_shapes=[
            pltpu.VMEM((3, 16, 512), BF16),
            pltpu.VMEM((3, 16, 512), BF16),
            pltpu.SemaphoreType.DMA((3,)),
            pltpu.SemaphoreType.DMA((8,)),
        ],
        compiler_params=pltpu.CompilerParams(vmem_limit_bytes=8 << 20),
        name="renorm",
    )(rank, recv, wg, wu, wd)


def attend_kernel(
    pos_ref, doc_ref, q_hbm, k_hbm, v_hbm, wc_hbm, pk1, pv1, pk2, pv2, out_ref, q_ref, wc_ref,
    k_ref, v_ref, pk_ref, pv_ref, sem,
):
    base = pos_ref[0]
    first = pos_ref[1] == 1
    loads = [
        pltpu.make_async_copy(src, dst, sem.at[i + 2])
        for i, (src, dst) in enumerate(
            ((q_hbm, q_ref), (k_hbm, k_ref), (v_hbm, v_ref), (wc_hbm, wc_ref))
        )
    ]
    for load in loads:
        load.start()

    @pl.when(first)
    def _():
        pltpu.make_async_copy(pk1, pk_ref, sem.at[0]).start()
        pltpu.make_async_copy(pv1, pv_ref, sem.at[1]).start()

    @pl.when(jnp.logical_not(first))
    def _():
        pltpu.make_async_copy(pk2, pk_ref, sem.at[0]).start()
        pltpu.make_async_copy(pv2, pv_ref, sem.at[1]).start()

    pltpu.make_async_copy(pk1, pk_ref, sem.at[0]).wait()
    pltpu.make_async_copy(pv1, pv_ref, sem.at[1]).wait()
    for load in loads:
        load.wait()
    step = 128
    scale = 1.0 / math.sqrt(512)
    doc = (jnp.broadcast_to(doc_ref[...], (8, 512)) - base).T[:, :1]
    for start in range(0, 512, step):
        rows = slice(start, start + step)
        q = q_ref[0, rows, :]
        keys = jnp.concatenate([pk_ref[0, start:, :], k_ref[0, : start + step, :]], axis=0)
        vals = jnp.concatenate([pv_ref[0, start:, :], v_ref[0, : start + step, :]], axis=0)
        width = 512 + step
        s = dot(q, keys, NT) * scale
        at = lax.broadcasted_iota(jnp.int32, (step, width), 0) + start
        to = lax.broadcasted_iota(jnp.int32, (step, width), 1) + (start - 512)
        ok = (to <= at) & (to > at - 512) & (to >= doc[rows])
        s = jnp.where(ok, s, -1e30)
        top = jnp.max(s, axis=-1, keepdims=True)
        e = jnp.exp(s - top)
        prob = (e / jnp.sum(e, axis=-1, keepdims=True)).astype(BF16)
        out_ref[rows, :] = dot(prob, vals, NN)


def attend(pos, q, k, v, doc, wc, pk1, pv1, pk2, pv2):
    vm = pl.BlockSpec(memory_space=pltpu.VMEM)
    hb = pl.BlockSpec(memory_space=pltpu.HBM)
    return pl.pallas_call(
        attend_kernel,
        out_shape=(
            jax.ShapeDtypeStruct((512, 512), F32),
            jax.ShapeDtypeStruct((1, 512, 512), BF16),
            jax.ShapeDtypeStruct((512, 512), BF16),
        ),
        in_specs=[pl.BlockSpec(memory_space=pltpu.SMEM), vm] + [hb] * 8,
        out_specs=(vm, vm, vm),
        scratch_shapes=[pltpu.VMEM((1, 512, 512), BF16)] * 4 + [pltpu.SemaphoreType.DMA((6,))],
        compiler_params=pltpu.CompilerParams(vmem_limit_bytes=20 << 20),
        name="attend",
    )(pos, doc, q, k, v, wc, pk1, pv1, pk2, pv2)


def relay_kernel(pos_ref, recv, wg, wu, wd, out, own, sem_in, sem_out):
    first = pos_ref[0] == 1
    column = pos_ref[1]

    @pl.when(first)
    def _():
        copies = []
        for i, ref in enumerate((wg, wu, wd)):
            for z in range(4):
                rows = pl.ds(pl.multiple_of((z * 8 + column) * 16, 16), 16)
                copies.append(pltpu.make_async_copy(ref.at[0, rows], own.at[z, i], sem_in.at[i, z]))
        for copy in copies:
            copy.start()
        for copy in copies:
            copy.wait()
        copies = [pltpu.make_async_copy(own, out.at[d], sem_out.at[d]) for d in range(8)]
        for copy in copies:
            copy.start()
        for copy in copies:
            copy.wait()

    @pl.when(jnp.logical_not(first))
    def _():
        copies = [
            pltpu.make_async_copy(recv.at[pl.ds(0, 4)], out.at[d], sem_out.at[d]) for d in range(8)
        ]
        for copy in copies:
            copy.start()
        for copy in copies:
            copy.wait()


def relay(pos, recv, wg, wu, wd):
    hb = pl.BlockSpec(memory_space=pltpu.HBM)
    return pl.pallas_call(
        relay_kernel,
        out_shape=jax.ShapeDtypeStruct((8, 4, 3, 16, 512), BF16),
        in_specs=[
            pl.BlockSpec(memory_space=pltpu.SMEM),
            pl.BlockSpec(memory_space=pltpu.VMEM),
            hb,
            hb,
            hb,
        ],
        out_specs=hb,
        scratch_shapes=[
            pltpu.VMEM((4, 3, 16, 512), BF16),
            pltpu.SemaphoreType.DMA((3, 4)),
            pltpu.SemaphoreType.DMA((8,)),
        ],
        compiler_params=pltpu.CompilerParams(vmem_limit_bytes=4 << 20),
        name="relay",
    )(pos, recv, wg, wu, wd)


def apply_kernel(
    fresh, att_s, q_s, wc_s, mixed_hbm, part_hbm, mixed_s, part_s, sem_out
):

    def weight(i, low, count):
        return jnp.concatenate(
            [fresh[y, z, i] for z in range(low // 128, (low + count) // 128) for y in range(8)], axis=0
        )

    step = APPLY_STEP
    q = q_s[0]
    hidden = []
    for start in range(0, 512, step):
        gate = dot(q, weight(0, start, step), NT)
        up = dot(q, weight(1, start, step), NT)
        hidden.append((gate * jax.nn.sigmoid(gate) * up).astype(BF16))
    hidden = jnp.concatenate(hidden, axis=1)
    for start in range(0, 512, step):
        cols = slice(start, start + step)
        mixed_s[:, cols] = (att_s[:, cols] + dot(hidden, weight(2, start, step), NT)).astype(BF16)
    stores = [pltpu.make_async_copy(mixed_s, mixed_hbm.at[0], sem_out.at[0])]
    stores[0].start()
    mixed = mixed_s[...]
    for start in range(0, 512, step):
        cols = slice(start, start + step)
        part_s[:, cols] = dot(mixed, wc_s[:, cols], NN).astype(BF16)
    stores.append(pltpu.make_async_copy(part_s, part_hbm, sem_out.at[1]))
    stores[1].start()
    for store in stores:
        store.wait()


def fast_apply(fresh, q, att, wc):
    vm = pl.BlockSpec(memory_space=pltpu.VMEM)
    hb = pl.BlockSpec(memory_space=pltpu.HBM)
    return pl.pallas_call(
        apply_kernel,
        out_shape=(
            jax.ShapeDtypeStruct((1, 512, 512), BF16),
            jax.ShapeDtypeStruct((512, 512), BF16),
        ),
        in_specs=[vm] * 4,
        out_specs=(hb, hb),
        scratch_shapes=[
            pltpu.VMEM((512, 512), BF16),
            pltpu.VMEM((512, 512), BF16),
            pltpu.SemaphoreType.DMA((2,)),
        ],
        compiler_params=pltpu.CompilerParams(vmem_limit_bytes=24 << 20),
        name="fast_apply",
    )(fresh, att, q, wc)


def combine_kernel(recv_ref, flag_ref, out_ref):
    summed = jnp.sum(recv_ref[...].astype(F32), axis=0)
    flag = jnp.broadcast_to(flag_ref[...].astype(F32), (8, 64)).T[:, :1]
    out_ref[0] = (summed * flag).astype(BF16)


def combine(recv, flag):
    vm = pl.BlockSpec(memory_space=pltpu.VMEM)
    return pl.pallas_call(
        combine_kernel,
        out_shape=jax.ShapeDtypeStruct((1, 64, 512), BF16),
        in_specs=[vm, vm],
        out_specs=vm,
        compiler_params=pltpu.CompilerParams(vmem_limit_bytes=4 << 20),
        name="combine",
    )(recv, flag)


def layer(q, k, v, rate, doc_start, flag, wg, wu, wd, wc):
    seq_count = lax.axis_size("seq")
    half = seq_count // 2
    index = lax.axis_index("seq")
    first = (index < half).astype(jnp.int32)
    rank = lax.rem(index, half)
    halves = [list(range(half)), list(range(half, seq_count))]
    ygroups = [[z * 8 + y for y in range(8)] for z in range(8)]
    zgroups = [[z * 8 + y for z in range(8)] for y in range(8)]
    early = [(i - 1, i) for i in range(half, seq_count)]
    late = [(i - 1, i) for i in range(1, half)]

    pk2 = lax.ppermute(k, "seq", early)
    pv2 = lax.ppermute(v, "seq", early)
    terms = grads(k, v, rate, flag[None], wg, wu, wd)
    recv = lax.all_to_all(terms, "seq", 0, 0, axis_index_groups=halves)
    shard = renorm(rank[None].astype(jnp.int32), recv, wg, wu, wd, 512 * half)
    pk1 = lax.ppermute(k, "seq", late)
    pv1 = lax.ppermute(v, "seq", late)
    column = lax.all_to_all(shard, "seq", 0, 0, axis_index_groups=zgroups)
    spot = jnp.stack([first, lax.rem(index, 8).astype(jnp.int32)])
    column = relay(spot, column, wg, wu, wd)
    fresh = lax.all_to_all(column, "seq", 0, 0, axis_index_groups=ygroups)
    pos = jnp.stack([index.astype(jnp.int32) * 512, first])
    att, q_near, wc_near = attend(pos, q, k, v, doc_start[None], wc, pk1, pv1, pk2, pv2)
    mixed, part = fast_apply(fresh, q_near, att, wc_near)
    got = lax.all_to_all(part.reshape(8, 64, 512), "head", 0, 0)
    flags = lax.dynamic_slice_in_dim(flag, lax.axis_index("head") * 64, 64, 0)
    return mixed, combine(got, flags[None])


def solution(mesh):
    placed = (
        P("head", "seq", None),
        P("head", "seq", None),
        P("head", "seq", None),
        P("head", "seq"),
        P("seq"),
        P("seq"),
        P("head", None, None),
        P("head", None, None),
        P("head", None, None),
        P("head", None),
    )
    return jax.shard_map(
        layer,
        mesh=mesh,
        in_specs=placed,
        out_specs=(P("head", "seq", None), P("seq", "head", None)),
        check_vma=False,
    )
```

```python
import functools
import math
import jax
import jax.numpy as jnp
from jax import lax
from jax.experimental import pallas as pl
from jax.experimental.pallas import tpu as pltpu
from jax.sharding import PartitionSpec as P


F32 = jnp.float32
GRADS_STEP = 256
APPLY_STEP = 256
RENORM_VMEM = 51200 << 10
RELAY_VMEM = 54800 << 10
APPLY_VMEM = 50800 << 10
BF16 = jnp.bfloat16
NN = (((1,), (0,)), ((), ()))
NT = (((1,), (1,)), ((), ()))


def dot(a, b, dims):
    return lax.dot_general(a, b, dims, preferred_element_type=F32)


def grads_kernel(
    k_hbm, v_hbm, wg_hbm, wu_hbm, wd_hbm, rate_ref, flag_ref, out_hbm, kv_hbm,
    k_s, v_s, wg_s, wu_s, wd_s, out_s, sem_in, sem_out, sem_kv,
):
    loads = [
        pltpu.make_async_copy(src.at[0], dst, sem_in.at[i])
        for i, (src, dst) in enumerate(
            ((v_hbm, v_s), (wd_hbm, wd_s), (k_hbm, k_s), (wg_hbm, wg_s), (wu_hbm, wu_s))
        )
    ]
    for load in loads:
        load.start()
    step = GRADS_STEP
    part = step // 16
    stores = []

    def put(piece, which, start):
        for c in range(4):
            block = piece[:, c * 128 : (c + 1) * 128].reshape(part, 16, 128)
            row = which * 64 + c * 16
            out_s[start // 16 : start // 16 + part, row : row + 16, :] = block

    def ship(low, high, start, rows):
        window = (slice(start // 16, (start + rows) // 16), slice(low, high))
        store = pltpu.make_async_copy(out_s.at[window], out_hbm.at[window], sem_out.at[len(stores)])
        store.start()
        stores.append(store)

    rate = rate_ref[...]
    coeff = flag_ref[...].astype(F32) * rate
    total = jnp.sum(rate, axis=1, keepdims=True)
    high = total.astype(BF16)
    low = (total - high.astype(F32)).astype(BF16)
    row = lax.broadcasted_iota(jnp.int32, (8, 128), 0)
    tail = jnp.where(row == 0, high.astype(F32), jnp.where(row == 1, low.astype(F32), 0.0))
    out_s[:, 192:200, :] = jnp.broadcast_to(tail.astype(BF16)[None], (32, 8, 128))
    loads[0].wait()
    scaled = (coeff * v_s[...].T.astype(F32)).astype(BF16)
    loads[1].wait()
    down = wd_s[...].T
    for load in loads[2:]:
        load.wait()
    pair = [
        pltpu.make_async_copy(src, kv_hbm.at[i], sem_kv.at[i]) for i, src in enumerate((k_s, v_s))
    ]
    for copy in pair:
        copy.start()
    key = k_s[...]
    hidden = []
    for start in range(0, 512, step):
        rows = slice(start, start + step)
        gate = dot(wg_s[rows, :], key, NT)
        up = dot(wu_s[rows, :], key, NT)
        back = dot(down[rows], scaled, NN)
        sigma = jax.nn.sigmoid(gate)
        active = gate * sigma
        hidden.append((active * up).astype(BF16))
        grad_gate = (back * up * sigma * (1.0 + gate * (1.0 - sigma))).astype(BF16)
        grad_up = (back * active).astype(BF16)
        put(dot(grad_gate, key, NN).astype(BF16), 0, start)
        put(dot(grad_up, key, NN).astype(BF16), 1, start)
        ship(0, 128, start, step)
    hidden = jnp.concatenate(hidden, axis=0)
    for start in range(0, 512, step):
        rows = slice(start, start + step)
        put(dot(scaled[rows], hidden, NT).astype(BF16), 2, start)
        ship(128, 200, start, step)
    for store in stores + pair:
        store.wait()


def grads(k, v, rate, flag, wg, wu, wd):
    vm = pl.BlockSpec(memory_space=pltpu.VMEM)
    hb = pl.BlockSpec(memory_space=pltpu.HBM)
    return pl.pallas_call(
        grads_kernel,
        out_shape=(
            jax.ShapeDtypeStruct((32, 200, 128), BF16),
            jax.ShapeDtypeStruct((2, 512, 512), BF16),
        ),
        in_specs=[hb] * 5 + [vm, vm],
        out_specs=(hb, hb),
        scratch_shapes=[pltpu.VMEM((512, 512), BF16)] * 5
        + [
            pltpu.VMEM((32, 200, 128), BF16),
            pltpu.SemaphoreType.DMA((5,)),
            pltpu.SemaphoreType.DMA((2 * (512 // GRADS_STEP),)),
            pltpu.SemaphoreType.DMA((2,)),
        ],
        name="grads",
    )(k, v, wg, wu, wd, rate, flag)


def renorm_kernel(
    rank_ref, recv_ref, wg, wu, wd, out, old_s, new_s, sem_in, sem_out, *, update_len
):
    rows = pl.ds(pl.multiple_of(rank_ref[0] * 16, 16), 16)
    loads = [
        pltpu.make_async_copy(ref.at[0, rows], old_s.at[i], sem_in.at[i])
        for i, ref in enumerate((wg, wu, wd))
    ]
    for load in loads:
        load.start()
    tail = jnp.sum(recv_ref[:, 192:200, :].astype(F32), axis=0)
    total = tail[0:1, 0:1] + tail[1:2, 0:1]
    factor = 2.0 * update_len / (total * math.sqrt(update_len * 512))
    for which in range(3):
        pieces = []
        for c in range(4):
            row = which * 64 + c * 16
            pieces.append(jnp.sum(recv_ref[:, row : row + 16, :].astype(F32), axis=0))
        summed = jnp.concatenate(pieces, axis=1)
        loads[which].wait()
        old = old_s[which].astype(F32)
        updated = old + summed * factor
        old_norm = jnp.sqrt(jnp.sum(old * old, axis=-1, keepdims=True))
        new_norm = jnp.sqrt(jnp.sum(updated * updated, axis=-1, keepdims=True) + 1e-6)
        new_s[which] = (updated * (old_norm / new_norm)).astype(BF16)
    stores = [pltpu.make_async_copy(new_s, out.at[d], sem_out.at[d]) for d in range(8)]
    for store in stores:
        store.start()
    for store in stores:
        store.wait()


def renorm(rank, recv, wg, wu, wd, update_len):
    hb = pl.BlockSpec(memory_space=pltpu.HBM)
    return pl.pallas_call(
        functools.partial(renorm_kernel, update_len=update_len),
        out_shape=jax.ShapeDtypeStruct((8, 3, 16, 512), BF16),
        in_specs=[
            pl.BlockSpec(memory_space=pltpu.SMEM),
            pl.BlockSpec(memory_space=pltpu.VMEM),
            hb,
            hb,
            hb,
        ],
        out_specs=hb,
        scratch_shapes=[
            pltpu.VMEM((3, 16, 512), BF16),
            pltpu.VMEM((3, 16, 512), BF16),
            pltpu.SemaphoreType.DMA((3,)),
            pltpu.SemaphoreType.DMA((8,)),
        ],
        compiler_params=pltpu.CompilerParams(vmem_limit_bytes=RENORM_VMEM),
        name="renorm",
    )(rank, recv, wg, wu, wd)


def attend_kernel(
    pos_ref, doc_ref, q_hbm, k_hbm, v_hbm, prev_hbm, out_hbm, q_ref, k_ref, v_ref, prev, att_s, sem
):
    base = pos_ref[2]
    loads = [
        pltpu.make_async_copy(src.at[0], dst, sem.at[i])
        for i, (src, dst) in enumerate(((q_hbm, q_ref), (k_hbm, k_ref), (v_hbm, v_ref)))
    ]
    for load in loads:
        load.start()

    loads.append(pltpu.make_async_copy(prev_hbm, prev, sem.at[3]))
    loads[3].start()
    for load in loads:
        load.wait()
    step = 128
    scale = 1.0 / math.sqrt(512)
    doc = (jnp.broadcast_to(doc_ref[...], (8, 512)) - base).T[:, :1]
    for start in range(0, 512, step):
        rows = slice(start, start + step)
        q = q_ref[rows, :]
        keys = jnp.concatenate([prev[0, start:, :], k_ref[: start + step, :]], axis=0)
        vals = jnp.concatenate([prev[1, start:, :], v_ref[: start + step, :]], axis=0)
        width = 512 + step
        s = dot(q, keys, NT) * scale
        at = lax.broadcasted_iota(jnp.int32, (step, width), 0) + start
        to = lax.broadcasted_iota(jnp.int32, (step, width), 1) + (start - 512)
        ok = (to <= at) & (to > at - 512) & (to >= doc[rows])
        s = jnp.where(ok, s, -1e30)
        top = jnp.max(s, axis=-1, keepdims=True)
        e = jnp.exp(s - top)
        prob = (e / jnp.sum(e, axis=-1, keepdims=True)).astype(BF16)
        att_s[rows, :] = dot(prob, vals, NN)
    store = pltpu.make_async_copy(att_s, out_hbm.at[0], sem.at[4])
    store.start()
    store.wait()


def attend(pos, q, k, v, doc, prev):
    vm = pl.BlockSpec(memory_space=pltpu.VMEM)
    hb = pl.BlockSpec(memory_space=pltpu.HBM)
    return pl.pallas_call(
        attend_kernel,
        out_shape=jax.ShapeDtypeStruct((2, 512, 512), F32),
        in_specs=[pl.BlockSpec(memory_space=pltpu.SMEM), vm] + [hb] * 4,
        out_specs=hb,
        scratch_shapes=[pltpu.VMEM((512, 512), BF16)] * 3
        + [
            pltpu.VMEM((2, 512, 512), BF16),
            pltpu.VMEM((512, 512), F32),
            pltpu.SemaphoreType.DMA((5,)),
        ],
        name="attend",
    )(pos, doc, q, k, v, prev)


def relay_kernel(spot_ref, recv, wg, wu, wd, out, own, sem_in, sem_out):
    first = spot_ref[0] == 1
    column = spot_ref[1]

    def send(source):
        copies = [pltpu.make_async_copy(source, out.at[d], sem_out.at[d]) for d in range(8)]
        for copy in copies:
            copy.start()
        for copy in copies:
            copy.wait()

    @pl.when(first)
    def _():
        copies = [
            pltpu.make_async_copy(ref.at[:, column], own.at[:, i], sem_in.at[i])
            for i, ref in enumerate((wg, wu, wd))
        ]
        for copy in copies:
            copy.start()
        for copy in copies:
            copy.wait()
        send(own)

    @pl.when(jnp.logical_not(first))
    def _():
        send(recv.at[pl.ds(0, 4)])


def relay(spot, recv, wg, wu, wd):
    vm = pl.BlockSpec(memory_space=pltpu.VMEM)
    hb = pl.BlockSpec(memory_space=pltpu.HBM)
    return pl.pallas_call(
        relay_kernel,
        out_shape=jax.ShapeDtypeStruct((8, 4, 3, 16, 512), BF16),
        in_specs=[pl.BlockSpec(memory_space=pltpu.SMEM), vm, hb, hb, hb],
        out_specs=hb,
        scratch_shapes=[
            pltpu.VMEM((4, 3, 16, 512), BF16),
            pltpu.SemaphoreType.DMA((3,)),
            pltpu.SemaphoreType.DMA((8,)),
        ],
        compiler_params=pltpu.CompilerParams(vmem_limit_bytes=RELAY_VMEM),
        name="relay",
    )(spot, recv, *(x.reshape(4, 8, 16, 512) for x in (wg, wu, wd)))


def apply_kernel(
    fresh, q_hbm, att_hbm, wc_hbm, mixed_hbm, part_hbm,
    q_s, att_s, wc_s, mixed_s, part_s, sem_in, sem_out,
):
    loads = [
        pltpu.make_async_copy(src, dst, sem_in.at[i])
        for i, (src, dst) in enumerate(((q_hbm.at[0], q_s), (att_hbm.at[0], att_s), (wc_hbm, wc_s)))
    ]
    for load in loads:
        load.start()

    def weight(i, low, count):
        spots = [(z, y) for z in range(low // 128, (low + count) // 128) for y in range(8)]
        return jnp.concatenate([fresh[y, z, i] for z, y in spots], axis=0)

    step = APPLY_STEP
    loads[0].wait()
    q = q_s[...]
    hidden = []
    for start in range(0, 512, step):
        gate = dot(q, weight(0, start, step), NT)
        up = dot(q, weight(1, start, step), NT)
        hidden.append((gate * jax.nn.sigmoid(gate) * up).astype(BF16))
    hidden = jnp.concatenate(hidden, axis=1)
    loads[1].wait()
    for start in range(0, 512, step):
        cols = slice(start, start + step)
        mixed_s[:, cols] = (att_s[:, cols] + dot(hidden, weight(2, start, step), NT)).astype(BF16)
    stores = [pltpu.make_async_copy(mixed_s, mixed_hbm.at[0], sem_out.at[0])]
    stores[0].start()
    loads[2].wait()
    mixed = mixed_s[...]
    for start in range(0, 512, step):
        cols = slice(start, start + step)
        part_s[:, cols] = dot(mixed, wc_s[:, cols], NN).astype(BF16)
    stores.append(pltpu.make_async_copy(part_s, part_hbm, sem_out.at[1]))
    stores[1].start()
    for store in stores:
        store.wait()


def fast_apply(fresh, q, att, wc):
    vm = pl.BlockSpec(memory_space=pltpu.VMEM)
    hb = pl.BlockSpec(memory_space=pltpu.HBM)
    return pl.pallas_call(
        apply_kernel,
        out_shape=(
            jax.ShapeDtypeStruct((1, 512, 512), BF16),
            jax.ShapeDtypeStruct((512, 512), BF16),
        ),
        in_specs=[vm, hb, hb, hb],
        out_specs=(hb, hb),
        scratch_shapes=[
            pltpu.VMEM((512, 512), BF16),
            pltpu.VMEM((512, 512), F32),
            pltpu.VMEM((512, 512), BF16),
            pltpu.VMEM((512, 512), BF16),
            pltpu.VMEM((512, 512), BF16),
            pltpu.SemaphoreType.DMA((3,)),
            pltpu.SemaphoreType.DMA((2,)),
        ],
        compiler_params=pltpu.CompilerParams(vmem_limit_bytes=APPLY_VMEM),
        name="fast_apply",
    )(fresh, q, att, wc)


def combine_kernel(recv_ref, flag_ref, out_ref):
    summed = jnp.sum(recv_ref[...].astype(F32), axis=0)
    flag = jnp.broadcast_to(flag_ref[...].astype(F32), (8, 64)).T[:, :1]
    out_ref[0] = (summed * flag).astype(BF16)


def combine(recv, flag):
    vm = pl.BlockSpec(memory_space=pltpu.VMEM)
    return pl.pallas_call(
        combine_kernel,
        out_shape=jax.ShapeDtypeStruct((1, 64, 512), BF16),
        in_specs=[vm, vm],
        out_specs=vm,
        compiler_params=pltpu.CompilerParams(vmem_limit_bytes=4 << 20),
        name="combine",
    )(recv, flag)


def mark_kernel(x_ref, out_ref):
    out_ref[...] = x_ref[...]


def mark(x):
    vm = pl.BlockSpec(memory_space=pltpu.VMEM)
    return pl.pallas_call(
        mark_kernel,
        out_shape=jax.ShapeDtypeStruct(x.shape, x.dtype),
        in_specs=[vm],
        out_specs=vm,
    )(x)


def layer(q, k, v, rate, doc_start, flag, wg, wu, wd, wc):
    seq_count = lax.axis_size("seq")
    half = seq_count // 2
    index = lax.axis_index("seq").astype(jnp.int32)
    first = (index < half).astype(jnp.int32)
    rank = lax.rem(index, half)
    halves = [list(range(half)), list(range(half, seq_count))]
    columns = [[z * 8 + y for z in range(8)] for y in range(8)]
    rows = [[z * 8 + y for y in range(8)] for z in range(8)]
    route = [(i - 1, i) for i in range(1, seq_count)]

    flags = lax.dynamic_slice_in_dim(flag, lax.axis_index("head") * 64, 64, 0)[None]
    flags = mark(flags)
    spot = jnp.stack([first, lax.rem(index, 8), index * 512])
    terms, kv = grads(k, v, rate, flag[None], wg, wu, wd)
    recv = lax.all_to_all(terms, "seq", 0, 0, axis_index_groups=halves)
    prev = lax.ppermute(kv, "seq", route)
    shard = renorm(rank[None], recv, wg, wu, wd, 512 * half)
    shard = lax.all_to_all(shard, "seq", 0, 0, axis_index_groups=columns)
    shard = relay(spot, shard, wg, wu, wd)
    fresh = lax.all_to_all(shard, "seq", 0, 0, axis_index_groups=rows)
    att = attend(spot, q, k, v, doc_start[None], prev)
    mixed, part = fast_apply(fresh, q, att, wc)
    got = lax.all_to_all(part.reshape(8, 64, 512), "head", 0, 0)
    return mixed, combine(got, flags)


def solution(mesh):
    placed = (
        P("head", "seq", None),
        P("head", "seq", None),
        P("head", "seq", None),
        P("head", "seq"),
        P("seq"),
        P("seq"),
        P("head", None, None),
        P("head", None, None),
        P("head", None, None),
        P("head", None),
    )
    return jax.shard_map(
        layer,
        mesh=mesh,
        in_specs=placed,
        out_specs=(P("head", "seq", None), P("seq", "head", None)),
        check_vma=False,
    )
```

```python
import functools
import math
import jax
import jax.numpy as jnp
from jax import lax
from jax.experimental import pallas as pl
from jax.experimental.pallas import tpu as pltpu
from jax.sharding import PartitionSpec as P


F32 = jnp.float32
GRADS_STEP = 256
APPLY_STEP = 256
RENORM_VMEM = 51200 << 10
RELAY_VMEM = 54800 << 10
APPLY_VMEM = 50800 << 10
BF16 = jnp.bfloat16
NN = (((1,), (0,)), ((), ()))
NT = (((1,), (1,)), ((), ()))


def dot(a, b, dims):
    return lax.dot_general(a, b, dims, preferred_element_type=F32)


def grads_kernel(
    k_hbm, v_hbm, wg_hbm, wu_hbm, wd_hbm, rate_ref, flag_ref, out_hbm,
    k_s, v_s, wg_s, wu_s, wd_s, out_s, sem_in, sem_out,
):
    loads = [
        pltpu.make_async_copy(src.at[0], dst, sem_in.at[i])
        for i, (src, dst) in enumerate(
            ((v_hbm, v_s), (wd_hbm, wd_s), (k_hbm, k_s), (wg_hbm, wg_s), (wu_hbm, wu_s))
        )
    ]
    for load in loads:
        load.start()
    step = GRADS_STEP
    part = step // 16
    stores = []

    def put(piece, which, start):
        for c in range(4):
            block = piece[:, c * 128 : (c + 1) * 128].reshape(part, 16, 128)
            row = which * 64 + c * 16
            out_s[start // 16 : start // 16 + part, row : row + 16, :] = block

    def ship(low, high, start, rows):
        window = (slice(start // 16, (start + rows) // 16), slice(low, high))
        store = pltpu.make_async_copy(out_s.at[window], out_hbm.at[window], sem_out.at[len(stores)])
        store.start()
        stores.append(store)

    rate = rate_ref[...]
    coeff = flag_ref[...].astype(F32) * rate
    total = jnp.sum(rate, axis=1, keepdims=True)
    high = total.astype(BF16)
    low = (total - high.astype(F32)).astype(BF16)
    row = lax.broadcasted_iota(jnp.int32, (8, 128), 0)
    tail = jnp.where(row == 0, high.astype(F32), jnp.where(row == 1, low.astype(F32), 0.0))
    out_s[:, 192:200, :] = jnp.broadcast_to(tail.astype(BF16)[None], (32, 8, 128))
    loads[0].wait()
    scaled = (coeff * v_s[...].T.astype(F32)).astype(BF16)
    loads[1].wait()
    down = wd_s[...].T
    for load in loads[2:]:
        load.wait()
    key = k_s[...]
    hidden = []
    for start in range(0, 512, step):
        rows = slice(start, start + step)
        gate = dot(wg_s[rows, :], key, NT)
        up = dot(wu_s[rows, :], key, NT)
        back = dot(down[rows], scaled, NN)
        sigma = jax.nn.sigmoid(gate)
        active = gate * sigma
        hidden.append((active * up).astype(BF16))
        grad_gate = (back * up * sigma * (1.0 + gate * (1.0 - sigma))).astype(BF16)
        grad_up = (back * active).astype(BF16)
        put(dot(grad_gate, key, NN).astype(BF16), 0, start)
        put(dot(grad_up, key, NN).astype(BF16), 1, start)
        ship(0, 128, start, step)
    hidden = jnp.concatenate(hidden, axis=0)
    for start in range(0, 512, step):
        rows = slice(start, start + step)
        put(dot(scaled[rows], hidden, NT).astype(BF16), 2, start)
        ship(128, 200, start, step)
    for store in stores:
        store.wait()


def grads(k, v, rate, flag, wg, wu, wd):
    vm = pl.BlockSpec(memory_space=pltpu.VMEM)
    hb = pl.BlockSpec(memory_space=pltpu.HBM)
    return pl.pallas_call(
        grads_kernel,
        out_shape=jax.ShapeDtypeStruct((32, 200, 128), BF16),
        in_specs=[hb] * 5 + [vm, vm],
        out_specs=hb,
        scratch_shapes=[pltpu.VMEM((512, 512), BF16)] * 5
        + [
            pltpu.VMEM((32, 200, 128), BF16),
            pltpu.SemaphoreType.DMA((5,)),
            pltpu.SemaphoreType.DMA((2 * (512 // GRADS_STEP),)),
        ],
        name="grads",
    )(k, v, wg, wu, wd, rate, flag)


def renorm_kernel(
    rank_ref, recv_ref, wg, wu, wd, out, old_s, new_s, sem_in, sem_out, *, update_len
):
    rows = pl.ds(pl.multiple_of(rank_ref[0] * 16, 16), 16)
    loads = [
        pltpu.make_async_copy(ref.at[0, rows], old_s.at[i], sem_in.at[i])
        for i, ref in enumerate((wg, wu, wd))
    ]
    for load in loads:
        load.start()
    tail = jnp.sum(recv_ref[:, 192:200, :].astype(F32), axis=0)
    total = tail[0:1, 0:1] + tail[1:2, 0:1]
    factor = 2.0 * update_len / (total * math.sqrt(update_len * 512))
    for which in range(3):
        pieces = []
        for c in range(4):
            row = which * 64 + c * 16
            pieces.append(jnp.sum(recv_ref[:, row : row + 16, :].astype(F32), axis=0))
        summed = jnp.concatenate(pieces, axis=1)
        loads[which].wait()
        old = old_s[which].astype(F32)
        updated = old + summed * factor
        old_norm = jnp.sqrt(jnp.sum(old * old, axis=-1, keepdims=True))
        new_norm = jnp.sqrt(jnp.sum(updated * updated, axis=-1, keepdims=True) + 1e-6)
        new_s[which] = (updated * (old_norm / new_norm)).astype(BF16)
    stores = [pltpu.make_async_copy(new_s, out.at[d], sem_out.at[d]) for d in range(8)]
    for store in stores:
        store.start()
    for store in stores:
        store.wait()


def renorm(rank, recv, wg, wu, wd, update_len):
    hb = pl.BlockSpec(memory_space=pltpu.HBM)
    return pl.pallas_call(
        functools.partial(renorm_kernel, update_len=update_len),
        out_shape=jax.ShapeDtypeStruct((8, 3, 16, 512), BF16),
        in_specs=[
            pl.BlockSpec(memory_space=pltpu.SMEM),
            pl.BlockSpec(memory_space=pltpu.VMEM),
            hb,
            hb,
            hb,
        ],
        out_specs=hb,
        scratch_shapes=[
            pltpu.VMEM((3, 16, 512), BF16),
            pltpu.VMEM((3, 16, 512), BF16),
            pltpu.SemaphoreType.DMA((3,)),
            pltpu.SemaphoreType.DMA((8,)),
        ],
        compiler_params=pltpu.CompilerParams(vmem_limit_bytes=RENORM_VMEM),
        name="renorm",
    )(rank, recv, wg, wu, wd)


def attend_kernel(
    pos_ref, doc_ref, q_hbm, k_hbm, v_hbm, pk_hbm, pv_hbm, out_hbm,
    q_ref, k_ref, v_ref, pk_ref, pv_ref, att_s, sem,
):
    base = pos_ref[2]
    loads = [
        pltpu.make_async_copy(src.at[0], dst, sem.at[i])
        for i, (src, dst) in enumerate(
            (
                (q_hbm, q_ref),
                (k_hbm, k_ref),
                (v_hbm, v_ref),
                (pk_hbm, pk_ref),
                (pv_hbm, pv_ref),
            )
        )
    ]
    for load in loads:
        load.start()

    for load in loads:
        load.wait()
    step = 128
    scale = 1.0 / math.sqrt(512)
    doc = (jnp.broadcast_to(doc_ref[...], (8, 512)) - base).T[:, :1]
    for start in range(0, 512, step):
        rows = slice(start, start + step)
        q = q_ref[rows, :]
        keys = jnp.concatenate([pk_ref[start:, :], k_ref[: start + step, :]], axis=0)
        vals = jnp.concatenate([pv_ref[start:, :], v_ref[: start + step, :]], axis=0)
        width = 512 + step
        s = dot(q, keys, NT) * scale
        at = lax.broadcasted_iota(jnp.int32, (step, width), 0) + start
        to = lax.broadcasted_iota(jnp.int32, (step, width), 1) + (start - 512)
        ok = (to <= at) & (to > at - 512) & (to >= doc[rows])
        s = jnp.where(ok, s, -1e30)
        top = jnp.max(s, axis=-1, keepdims=True)
        e = jnp.exp(s - top)
        prob = (e / jnp.sum(e, axis=-1, keepdims=True)).astype(BF16)
        att_s[rows, :] = dot(prob, vals, NN)
    store = pltpu.make_async_copy(att_s, out_hbm.at[0], sem.at[5])
    store.start()
    store.wait()


def attend(pos, q, k, v, doc, pk, pv):
    vm = pl.BlockSpec(memory_space=pltpu.VMEM)
    hb = pl.BlockSpec(memory_space=pltpu.HBM)
    return pl.pallas_call(
        attend_kernel,
        out_shape=jax.ShapeDtypeStruct((2, 512, 512), F32),
        in_specs=[pl.BlockSpec(memory_space=pltpu.SMEM), vm] + [hb] * 5,
        out_specs=hb,
        scratch_shapes=[pltpu.VMEM((512, 512), BF16)] * 5
        + [
            pltpu.VMEM((512, 512), F32),
            pltpu.SemaphoreType.DMA((6,)),
        ],
        name="attend",
    )(pos, doc, q, k, v, pk, pv)


def relay_kernel(spot_ref, recv, wg, wu, wd, out, own, sem_in, sem_out):
    first = spot_ref[0] == 1
    column = spot_ref[1]

    def send(source):
        copies = [pltpu.make_async_copy(source, out.at[d], sem_out.at[d]) for d in range(8)]
        for copy in copies:
            copy.start()
        for copy in copies:
            copy.wait()

    @pl.when(first)
    def _():
        copies = [
            pltpu.make_async_copy(ref.at[:, column], own.at[:, i], sem_in.at[i])
            for i, ref in enumerate((wg, wu, wd))
        ]
        for copy in copies:
            copy.start()
        for copy in copies:
            copy.wait()
        send(own)

    @pl.when(jnp.logical_not(first))
    def _():
        send(recv.at[pl.ds(0, 4)])


def relay(spot, recv, wg, wu, wd):
    vm = pl.BlockSpec(memory_space=pltpu.VMEM)
    hb = pl.BlockSpec(memory_space=pltpu.HBM)
    return pl.pallas_call(
        relay_kernel,
        out_shape=jax.ShapeDtypeStruct((8, 4, 3, 16, 512), BF16),
        in_specs=[pl.BlockSpec(memory_space=pltpu.SMEM), vm, hb, hb, hb],
        out_specs=hb,
        scratch_shapes=[
            pltpu.VMEM((4, 3, 16, 512), BF16),
            pltpu.SemaphoreType.DMA((3,)),
            pltpu.SemaphoreType.DMA((8,)),
        ],
        compiler_params=pltpu.CompilerParams(vmem_limit_bytes=RELAY_VMEM),
        name="relay",
    )(spot, recv, *(x.reshape(4, 8, 16, 512) for x in (wg, wu, wd)))


def apply_kernel(
    fresh, q_hbm, att_hbm, wc_hbm, mixed_hbm, part_hbm,
    q_s, att_s, wc_s, mixed_s, part_s, sem_in, sem_out,
):
    loads = [
        pltpu.make_async_copy(src, dst, sem_in.at[i])
        for i, (src, dst) in enumerate(((q_hbm.at[0], q_s), (att_hbm.at[0], att_s), (wc_hbm, wc_s)))
    ]
    for load in loads:
        load.start()

    def weight(i, low, count):
        spots = [(z, y) for z in range(low // 128, (low + count) // 128) for y in range(8)]
        return jnp.concatenate([fresh[y, z, i] for z, y in spots], axis=0)

    step = APPLY_STEP
    loads[0].wait()
    q = q_s[...]
    hidden = []
    for start in range(0, 512, step):
        gate = dot(q, weight(0, start, step), NT)
        up = dot(q, weight(1, start, step), NT)
        hidden.append((gate * jax.nn.sigmoid(gate) * up).astype(BF16))
    hidden = jnp.concatenate(hidden, axis=1)
    loads[1].wait()
    for start in range(0, 512, step):
        cols = slice(start, start + step)
        mixed_s[:, cols] = (att_s[:, cols] + dot(hidden, weight(2, start, step), NT)).astype(BF16)
    stores = [pltpu.make_async_copy(mixed_s, mixed_hbm.at[0], sem_out.at[0])]
    stores[0].start()
    loads[2].wait()
    mixed = mixed_s[...]
    for start in range(0, 512, step):
        cols = slice(start, start + step)
        part_s[:, cols] = dot(mixed, wc_s[:, cols], NN).astype(BF16)
    stores.append(pltpu.make_async_copy(part_s, part_hbm, sem_out.at[1]))
    stores[1].start()
    for store in stores:
        store.wait()


def fast_apply(fresh, q, att, wc):
    vm = pl.BlockSpec(memory_space=pltpu.VMEM)
    hb = pl.BlockSpec(memory_space=pltpu.HBM)
    return pl.pallas_call(
        apply_kernel,
        out_shape=(
            jax.ShapeDtypeStruct((1, 512, 512), BF16),
            jax.ShapeDtypeStruct((512, 512), BF16),
        ),
        in_specs=[vm, hb, hb, hb],
        out_specs=(hb, hb),
        scratch_shapes=[
            pltpu.VMEM((512, 512), BF16),
            pltpu.VMEM((512, 512), F32),
            pltpu.VMEM((512, 512), BF16),
            pltpu.VMEM((512, 512), BF16),
            pltpu.VMEM((512, 512), BF16),
            pltpu.SemaphoreType.DMA((3,)),
            pltpu.SemaphoreType.DMA((2,)),
        ],
        compiler_params=pltpu.CompilerParams(vmem_limit_bytes=APPLY_VMEM),
        name="fast_apply",
    )(fresh, q, att, wc)


def combine_kernel(recv_ref, flag_ref, out_ref):
    summed = jnp.sum(recv_ref[...].astype(F32), axis=0)
    flag = jnp.broadcast_to(flag_ref[...].astype(F32), (8, 64)).T[:, :1]
    out_ref[0] = (summed * flag).astype(BF16)


def combine(recv, flag):
    vm = pl.BlockSpec(memory_space=pltpu.VMEM)
    return pl.pallas_call(
        combine_kernel,
        out_shape=jax.ShapeDtypeStruct((1, 64, 512), BF16),
        in_specs=[vm, vm],
        out_specs=vm,
        compiler_params=pltpu.CompilerParams(vmem_limit_bytes=4 << 20),
        name="combine",
    )(recv, flag)


def layer(q, k, v, rate, doc_start, flag, wg, wu, wd, wc):
    seq_count = lax.axis_size("seq")
    half = seq_count // 2
    index = lax.axis_index("seq").astype(jnp.int32)
    first = (index < half).astype(jnp.int32)
    rank = lax.rem(index, half)
    halves = [list(range(half)), list(range(half, seq_count))]
    columns = [[z * 8 + y for z in range(8)] for y in range(8)]
    rows = [[z * 8 + y for y in range(8)] for z in range(8)]
    route = [(i - 1, i) for i in range(1, seq_count)]

    flags = lax.dynamic_slice_in_dim(flag, lax.axis_index("head") * 64, 64, 0)[None]
    spot = jnp.stack([first, lax.rem(index, 8), index * 512])
    pk = lax.ppermute(k, "seq", route)
    pv = lax.ppermute(v, "seq", route)
    terms = grads(k, v, rate, flag[None], wg, wu, wd)
    recv = lax.all_to_all(terms, "seq", 0, 0, axis_index_groups=halves)
    shard = renorm(rank[None], recv, wg, wu, wd, 512 * half)
    shard = lax.all_to_all(shard, "seq", 0, 0, axis_index_groups=columns)
    shard = relay(spot, shard, wg, wu, wd)
    fresh = lax.all_to_all(shard, "seq", 0, 0, axis_index_groups=rows)
    att = attend(spot, q, k, v, doc_start[None], pk, pv)
    mixed, part = fast_apply(fresh, q, att, wc)
    got = lax.all_to_all(part.reshape(8, 64, 512), "head", 0, 0)
    return mixed, combine(got, flags)


def solution(mesh):
    placed = (
        P("head", "seq", None),
        P("head", "seq", None),
        P("head", "seq", None),
        P("head", "seq"),
        P("seq"),
        P("seq"),
        P("head", None, None),
        P("head", None, None),
        P("head", None, None),
        P("head", None),
    )
    return jax.shard_map(
        layer,
        mesh=mesh,
        in_specs=placed,
        out_specs=(P("head", "seq", None), P("seq", "head", None)),
        check_vma=False,
    )
```

```python
import functools
import math
import jax
import jax.numpy as jnp
from jax import lax
from jax.experimental import pallas as pl
from jax.experimental.pallas import tpu as pltpu
from jax.sharding import PartitionSpec as P


F32 = jnp.float32
GRADS_STEP = 256
APPLY_STEP = 256
FOLD_VMEM = 52000 << 10
RENORM_VMEM = 52000 << 10
RELAY_VMEM = 54800 << 10
APPLY_VMEM = 50800 << 10
BF16 = jnp.bfloat16
NN = (((1,), (0,)), ((), ()))
NT = (((1,), (1,)), ((), ()))


def dot(a, b, dims):
    return lax.dot_general(a, b, dims, preferred_element_type=F32)


def grads_kernel(
    k_hbm, v_hbm, wg_hbm, wu_hbm, wd_hbm, rate_ref, flag_ref, out_hbm,
    k_s, v_s, wg_s, wu_s, wd_s, out_s, sem_in, sem_out,
):
    loads = [
        pltpu.make_async_copy(src.at[0], dst, sem_in.at[i])
        for i, (src, dst) in enumerate(
            ((v_hbm, v_s), (wd_hbm, wd_s), (k_hbm, k_s), (wg_hbm, wg_s), (wu_hbm, wu_s))
        )
    ]
    for load in loads:
        load.start()
    step = GRADS_STEP
    part = step // 16
    stores = []

    def put(piece, which, start):
        for c in range(4):
            block = piece[:, c * 128 : (c + 1) * 128].reshape(part, 16, 128)
            row = which * 64 + c * 16
            out_s[start // 16 : start // 16 + part, row : row + 16, :] = block

    def ship(low, high, start, rows):
        window = (slice(start // 16, (start + rows) // 16), slice(low, high))
        store = pltpu.make_async_copy(out_s.at[window], out_hbm.at[window], sem_out.at[len(stores)])
        store.start()
        stores.append(store)

    rate = rate_ref[...]
    coeff = flag_ref[...].astype(F32) * rate
    total = jnp.sum(rate, axis=1, keepdims=True)
    high = total.astype(BF16)
    low = (total - high.astype(F32)).astype(BF16)
    row = lax.broadcasted_iota(jnp.int32, (8, 128), 0)
    tail = jnp.where(row == 0, high.astype(F32), jnp.where(row == 1, low.astype(F32), 0.0))
    out_s[:, 192:200, :] = jnp.broadcast_to(tail.astype(BF16)[None], (32, 8, 128))
    loads[0].wait()
    scaled = (coeff * v_s[...].T.astype(F32)).astype(BF16)
    loads[1].wait()
    down = wd_s[...].T
    for load in loads[2:]:
        load.wait()
    key = k_s[...]
    hidden = []
    for start in range(0, 512, step):
        rows = slice(start, start + step)
        gate = dot(wg_s[rows, :], key, NT)
        up = dot(wu_s[rows, :], key, NT)
        back = dot(down[rows], scaled, NN)
        sigma = jax.nn.sigmoid(gate)
        active = gate * sigma
        hidden.append((active * up).astype(BF16))
        grad_gate = (back * up * sigma * (1.0 + gate * (1.0 - sigma))).astype(BF16)
        grad_up = (back * active).astype(BF16)
        put(dot(grad_gate, key, NN).astype(BF16), 0, start)
        put(dot(grad_up, key, NN).astype(BF16), 1, start)
        ship(0, 128, start, step)
    hidden = jnp.concatenate(hidden, axis=0)
    for start in range(0, 512, step):
        rows = slice(start, start + step)
        put(dot(scaled[rows], hidden, NT).astype(BF16), 2, start)
        ship(128, 200, start, step)
    for store in stores:
        store.wait()


def grads(k, v, rate, flag, wg, wu, wd):
    vm = pl.BlockSpec(memory_space=pltpu.VMEM)
    hb = pl.BlockSpec(memory_space=pltpu.HBM)
    return pl.pallas_call(
        grads_kernel,
        out_shape=jax.ShapeDtypeStruct((32, 200, 128), BF16),
        in_specs=[hb] * 5 + [vm, vm],
        out_specs=hb,
        scratch_shapes=[pltpu.VMEM((512, 512), BF16)] * 5
        + [
            pltpu.VMEM((32, 200, 128), BF16),
            pltpu.SemaphoreType.DMA((5,)),
            pltpu.SemaphoreType.DMA((2 * (512 // GRADS_STEP),)),
        ],
        name="grads",
    )(k, v, wg, wu, wd, rate, flag)


def fold_kernel(recv_ref, out_hbm, out_s, sem):
    for j in range(4):
        out_s[j, :192, :] = jnp.sum(recv_ref[:, j, :192, :].astype(F32), axis=0).astype(BF16)
    tail = jnp.sum(recv_ref[:, 0, 192:200, :].astype(F32), axis=0)
    total = jnp.broadcast_to(tail[0:1] + tail[1:2], (8, 128))
    high = total.astype(BF16).astype(F32)
    row = lax.broadcasted_iota(jnp.int32, (8, 128), 0)
    tail = jnp.where(row == 0, high, jnp.where(row == 1, total - high, 0.0)).astype(BF16)
    out_s[:, 192:200, :] = jnp.broadcast_to(tail[None], (4, 8, 128))
    store = pltpu.make_async_copy(out_s, out_hbm, sem)
    store.start()
    store.wait()


def fold(recv):
    return pl.pallas_call(
        fold_kernel,
        out_shape=jax.ShapeDtypeStruct((4, 200, 128), BF16),
        in_specs=[pl.BlockSpec(memory_space=pltpu.VMEM)],
        out_specs=pl.BlockSpec(memory_space=pltpu.HBM),
        scratch_shapes=[pltpu.VMEM((4, 200, 128), BF16), pltpu.SemaphoreType.DMA],
        compiler_params=pltpu.CompilerParams(vmem_limit_bytes=FOLD_VMEM),
        name="fold",
    )(recv)


def renorm_kernel(
    rank_ref, recv_ref, wg, wu, wd, out, old_s, new_s, sem_in, sem_out, *, update_len
):
    rows = pl.ds(pl.multiple_of(rank_ref[0] * 16, 16), 16)
    loads = [
        pltpu.make_async_copy(ref.at[0, rows], old_s.at[i], sem_in.at[i])
        for i, ref in enumerate((wg, wu, wd))
    ]
    for load in loads:
        load.start()
    tail = jnp.sum(recv_ref[:, 192:200, :].astype(F32), axis=0)
    total = tail[0:1, 0:1] + tail[1:2, 0:1]
    factor = 2.0 * update_len / (total * math.sqrt(update_len * 512))
    for which in range(3):
        pieces = []
        for c in range(4):
            row = which * 64 + c * 16
            pieces.append(jnp.sum(recv_ref[:, row : row + 16, :].astype(F32), axis=0))
        summed = jnp.concatenate(pieces, axis=1)
        loads[which].wait()
        old = old_s[which].astype(F32)
        updated = old + summed * factor
        old_norm = jnp.sqrt(jnp.sum(old * old, axis=-1, keepdims=True))
        new_norm = jnp.sqrt(jnp.sum(updated * updated, axis=-1, keepdims=True) + 1e-6)
        new_s[which] = (updated * (old_norm / new_norm)).astype(BF16)
    stores = [pltpu.make_async_copy(new_s, out.at[d], sem_out.at[d]) for d in range(8)]
    for store in stores:
        store.start()
    for store in stores:
        store.wait()


def renorm(rank, recv, wg, wu, wd, update_len):
    hb = pl.BlockSpec(memory_space=pltpu.HBM)
    return pl.pallas_call(
        functools.partial(renorm_kernel, update_len=update_len),
        out_shape=jax.ShapeDtypeStruct((8, 3, 16, 512), BF16),
        in_specs=[
            pl.BlockSpec(memory_space=pltpu.SMEM),
            pl.BlockSpec(memory_space=pltpu.VMEM),
            hb,
            hb,
            hb,
        ],
        out_specs=hb,
        scratch_shapes=[
            pltpu.VMEM((3, 16, 512), BF16),
            pltpu.VMEM((3, 16, 512), BF16),
            pltpu.SemaphoreType.DMA((3,)),
            pltpu.SemaphoreType.DMA((8,)),
        ],
        compiler_params=pltpu.CompilerParams(vmem_limit_bytes=RENORM_VMEM),
        name="renorm",
    )(rank, recv, wg, wu, wd)


def attend_kernel(
    pos_ref, doc_ref, q_hbm, k_hbm, v_hbm, pk_hbm, pv_hbm, out_hbm,
    q_ref, k_ref, v_ref, pk_ref, pv_ref, att_s, sem,
):
    base = pos_ref[2]
    loads = [
        pltpu.make_async_copy(src.at[0], dst, sem.at[i])
        for i, (src, dst) in enumerate(
            (
                (q_hbm, q_ref),
                (k_hbm, k_ref),
                (v_hbm, v_ref),
                (pk_hbm, pk_ref),
                (pv_hbm, pv_ref),
            )
        )
    ]
    for load in loads:
        load.start()

    for load in loads:
        load.wait()
    step = 128
    scale = 1.0 / math.sqrt(512)
    doc = (jnp.broadcast_to(doc_ref[...], (8, 512)) - base).T[:, :1]
    for start in range(0, 512, step):
        rows = slice(start, start + step)
        q = q_ref[rows, :]
        keys = jnp.concatenate([pk_ref[start:, :], k_ref[: start + step, :]], axis=0)
        vals = jnp.concatenate([pv_ref[start:, :], v_ref[: start + step, :]], axis=0)
        width = 512 + step
        s = dot(q, keys, NT) * scale
        at = lax.broadcasted_iota(jnp.int32, (step, width), 0) + start
        to = lax.broadcasted_iota(jnp.int32, (step, width), 1) + (start - 512)
        ok = (to <= at) & (to > at - 512) & (to >= doc[rows])
        s = jnp.where(ok, s, -1e30)
        top = jnp.max(s, axis=-1, keepdims=True)
        e = jnp.exp(s - top)
        prob = (e / jnp.sum(e, axis=-1, keepdims=True)).astype(BF16)
        att_s[rows, :] = dot(prob, vals, NN)
    store = pltpu.make_async_copy(att_s, out_hbm.at[0], sem.at[5])
    store.start()
    store.wait()


def attend(pos, q, k, v, doc, pk, pv):
    vm = pl.BlockSpec(memory_space=pltpu.VMEM)
    hb = pl.BlockSpec(memory_space=pltpu.HBM)
    return pl.pallas_call(
        attend_kernel,
        out_shape=jax.ShapeDtypeStruct((2, 512, 512), F32),
        in_specs=[pl.BlockSpec(memory_space=pltpu.SMEM), vm] + [hb] * 5,
        out_specs=hb,
        scratch_shapes=[pltpu.VMEM((512, 512), BF16)] * 5
        + [
            pltpu.VMEM((512, 512), F32),
            pltpu.SemaphoreType.DMA((6,)),
        ],
        name="attend",
    )(pos, doc, q, k, v, pk, pv)


def relay_kernel(spot_ref, recv, wg, wu, wd, out, own, sem_in, sem_out):
    first = spot_ref[0] == 1
    parity = spot_ref[1]
    pair = spot_ref[3]

    def send(source):
        copies = [pltpu.make_async_copy(source, out.at[d], sem_out.at[d]) for d in range(8)]
        for copy in copies:
            copy.start()
        for copy in copies:
            copy.wait()

    @pl.when(first)
    def _():
        copies = [
            pltpu.make_async_copy(ref.at[:, parity, pair], own.at[:, i], sem_in.at[i])
            for i, ref in enumerate((wg, wu, wd))
        ]
        for copy in copies:
            copy.start()
        for copy in copies:
            copy.wait()
        send(own)

    @pl.when(jnp.logical_not(first))
    def _():
        send(recv.at[pl.ds(0, 4)])


def relay(spot, recv, wg, wu, wd):
    vm = pl.BlockSpec(memory_space=pltpu.VMEM)
    hb = pl.BlockSpec(memory_space=pltpu.HBM)
    return pl.pallas_call(
        relay_kernel,
        out_shape=jax.ShapeDtypeStruct((8, 4, 3, 16, 512), BF16),
        in_specs=[pl.BlockSpec(memory_space=pltpu.SMEM), vm, hb, hb, hb],
        out_specs=hb,
        scratch_shapes=[
            pltpu.VMEM((4, 3, 16, 512), BF16),
            pltpu.SemaphoreType.DMA((3,)),
            pltpu.SemaphoreType.DMA((8,)),
        ],
        compiler_params=pltpu.CompilerParams(vmem_limit_bytes=RELAY_VMEM),
        name="relay",
    )(spot, recv, *(x.reshape(4, 2, 4, 16, 512) for x in (wg, wu, wd)))


def apply_kernel(
    fresh, q_hbm, att_hbm, wc_hbm, mixed_hbm, part_hbm,
    q_s, att_s, wc_s, mixed_s, part_s, sem_in, sem_out,
):
    loads = [
        pltpu.make_async_copy(src, dst, sem_in.at[i])
        for i, (src, dst) in enumerate(((q_hbm.at[0], q_s), (att_hbm.at[0], att_s), (wc_hbm, wc_s)))
    ]
    for load in loads:
        load.start()

    def weight(i, low, count):
        order = [(z, 2 * j + b) for z in range(4) for b in range(2) for j in range(4)]
        spots = order[low // 16 : (low + count) // 16]
        return jnp.concatenate([fresh[y, z, i] for z, y in spots], axis=0)

    step = APPLY_STEP
    loads[0].wait()
    q = q_s[...]
    hidden = []
    for start in range(0, 512, step):
        gate = dot(q, weight(0, start, step), NT)
        up = dot(q, weight(1, start, step), NT)
        hidden.append((gate * jax.nn.sigmoid(gate) * up).astype(BF16))
    hidden = jnp.concatenate(hidden, axis=1)
    loads[1].wait()
    for start in range(0, 512, step):
        cols = slice(start, start + step)
        mixed_s[:, cols] = (att_s[:, cols] + dot(hidden, weight(2, start, step), NT)).astype(BF16)
    stores = [pltpu.make_async_copy(mixed_s, mixed_hbm.at[0], sem_out.at[0])]
    stores[0].start()
    loads[2].wait()
    mixed = mixed_s[...]
    for start in range(0, 512, step):
        cols = slice(start, start + step)
        part_s[:, cols] = dot(mixed, wc_s[:, cols], NN).astype(BF16)
    stores.append(pltpu.make_async_copy(part_s, part_hbm, sem_out.at[1]))
    stores[1].start()
    for store in stores:
        store.wait()


def fast_apply(fresh, q, att, wc):
    vm = pl.BlockSpec(memory_space=pltpu.VMEM)
    hb = pl.BlockSpec(memory_space=pltpu.HBM)
    return pl.pallas_call(
        apply_kernel,
        out_shape=(
            jax.ShapeDtypeStruct((1, 512, 512), BF16),
            jax.ShapeDtypeStruct((512, 512), BF16),
        ),
        in_specs=[vm, hb, hb, hb],
        out_specs=(hb, hb),
        scratch_shapes=[
            pltpu.VMEM((512, 512), BF16),
            pltpu.VMEM((512, 512), F32),
            pltpu.VMEM((512, 512), BF16),
            pltpu.VMEM((512, 512), BF16),
            pltpu.VMEM((512, 512), BF16),
            pltpu.SemaphoreType.DMA((3,)),
            pltpu.SemaphoreType.DMA((2,)),
        ],
        compiler_params=pltpu.CompilerParams(vmem_limit_bytes=APPLY_VMEM),
        name="fast_apply",
    )(fresh, q, att, wc)


def combine_kernel(recv_ref, flag_ref, out_ref):
    summed = jnp.sum(recv_ref[...].astype(F32), axis=0)
    flag = jnp.broadcast_to(flag_ref[...].astype(F32), (8, 64)).T[:, :1]
    out_ref[0] = (summed * flag).astype(BF16)


def combine(recv, flag):
    vm = pl.BlockSpec(memory_space=pltpu.VMEM)
    return pl.pallas_call(
        combine_kernel,
        out_shape=jax.ShapeDtypeStruct((1, 64, 512), BF16),
        in_specs=[vm, vm],
        out_specs=vm,
        compiler_params=pltpu.CompilerParams(vmem_limit_bytes=4 << 20),
        name="combine",
    )(recv, flag)


def layer(q, k, v, rate, doc_start, flag, wg, wu, wd, wc):
    seq_count = lax.axis_size("seq")
    half = seq_count // 2
    index = lax.axis_index("seq").astype(jnp.int32)
    first = (index < half).astype(jnp.int32)
    z, y = lax.div(index, 8), lax.rem(index, 8)
    layer_z, parity, pair = lax.rem(z, 4), lax.rem(y, 2), lax.div(y, 2)
    place = lambda z, y: z * 8 + y
    blocks = [
        [place(z + lift, 2 * k + b) for z in range(4) for b in range(2)]
        for lift in (0, 4)
        for k in range(4)
    ]
    strides = [[place(z, 2 * j + b) for j in range(4)] for z in range(8) for b in range(2)]
    columns = [[place(z, y) for z in range(8)] for y in range(8)]
    rows = blocks[:4] + [[place(z, y) for y in range(8)] for z in range(4, 8)]
    route = [(i - 1, i) for i in range(1, seq_count)]

    spot_in_block = layer_z * 2 + parity
    sender = jnp.where(first == 1, spot_in_block, y)
    spot = jnp.stack([first, lax.rem(sender, 2), index * 512, lax.div(sender, 2)])
    pk = lax.ppermute(k, "seq", route)
    pv = lax.ppermute(v, "seq", route)
    terms = grads(k, v, rate, flag[None], wg, wu, wd)
    recv = lax.all_to_all(terms.reshape(8, 4, 200, 128), "seq", 0, 0, axis_index_groups=blocks)
    recv = lax.all_to_all(fold(recv), "seq", 0, 0, axis_index_groups=strides)
    rank = spot_in_block * 4 + pair
    shard = renorm(rank[None], recv, wg, wu, wd, 512 * half)
    shard = lax.all_to_all(shard, "seq", 0, 0, axis_index_groups=columns)
    shard = relay(spot, shard, wg, wu, wd)
    fresh = lax.all_to_all(shard, "seq", 0, 0, axis_index_groups=rows)
    att = attend(spot, q, k, v, doc_start[None], pk, pv)
    mixed, part = fast_apply(fresh, q, att, wc)
    flags = lax.dynamic_slice_in_dim(flag, lax.axis_index("head") * 64, 64, 0)[None]
    got = lax.all_to_all(part.reshape(8, 64, 512), "head", 0, 0)
    return mixed, combine(got, flags)


def solution(mesh):
    placed = (
        P("head", "seq", None),
        P("head", "seq", None),
        P("head", "seq", None),
        P("head", "seq"),
        P("seq"),
        P("seq"),
        P("head", None, None),
        P("head", None, None),
        P("head", None, None),
        P("head", None),
    )
    return jax.shard_map(
        layer,
        mesh=mesh,
        in_specs=placed,
        out_specs=(P("head", "seq", None), P("seq", "head", None)),
        check_vma=False,
    )
```

```python
import functools
import math
import jax
import jax.numpy as jnp
from jax import lax
from jax.experimental import pallas as pl
from jax.experimental.pallas import tpu as pltpu
from jax.sharding import PartitionSpec as P


F32 = jnp.float32
GRADS_STEP = 256
APPLY_STEP = 256
FOLD_VMEM = 53000 << 10
RENORM_VMEM = 53000 << 10
RELAY_VMEM = 53000 << 10
APPLY_VMEM = 50800 << 10
BF16 = jnp.bfloat16
NN = (((1,), (0,)), ((), ()))
NT = (((1,), (1,)), ((), ()))


def dot(a, b, dims):
    return lax.dot_general(a, b, dims, preferred_element_type=F32)


def grads_kernel(
    spot_ref, k_hbm, v_hbm, wg_hbm, wu_hbm, wd_hbm, rate_ref, flag_ref, left_hbm, *refs
):
    rights, (k_s, v_s, wg_s, wu_s, wd_s, left_s, right_s, sem_in, sem_left, sem_right) = refs[:4], refs[4:]
    layer_z = lax.rem(lax.div(spot_ref[0], 8), 4)
    loads = [
        pltpu.make_async_copy(src.at[0], dst, sem_in.at[i])
        for i, (src, dst) in enumerate(
            ((v_hbm, v_s), (wd_hbm, wd_s), (k_hbm, k_s), (wg_hbm, wg_s), (wu_hbm, wu_s))
        )
    ]
    for load in loads:
        load.start()
    step = GRADS_STEP
    stores = []

    def put(piece, which, start):
        for n in range(step // 16):
            z, y = divmod(start // 16 + n, 8)
            for c in range(4):
                block = piece[n * 16 : n * 16 + 16, c * 128 : (c + 1) * 128]
                row = which * 32 + (c % 2) * 16
                (left_s, right_s)[c // 2][z, y, row : row + 16, :] = block

    def ship(phase, low, high, top):
        for z in range(4):
            store = pltpu.make_async_copy(
                left_s.at[z, :, low:top], left_hbm.at[:, z, low:top], sem_left.at[phase, z]
            )
            store.start()
            stores.append(store)
        for d in range(4):
            store = pltpu.make_async_copy(
                right_s.at[lax.rem(layer_z + d, 4), :, low:high],
                rights[d].at[:, low:high],
                sem_right.at[phase, d],
            )
            store.start()
            stores.append(store)

    rate = rate_ref[...]
    coeff = flag_ref[...].astype(F32) * rate
    total = jnp.sum(rate, axis=1, keepdims=True)
    high = total.astype(BF16)
    low = (total - high.astype(F32)).astype(BF16)
    row = lax.broadcasted_iota(jnp.int32, (8, 128), 0)
    tail = jnp.where(row == 0, high.astype(F32), jnp.where(row == 1, low.astype(F32), 0.0))
    left_s[:, :, 96:104, :] = jnp.broadcast_to(tail.astype(BF16)[None, None], (4, 8, 8, 128))
    loads[0].wait()
    scaled = (coeff * v_s[...].T.astype(F32)).astype(BF16)
    loads[1].wait()
    down = wd_s[...].T
    for load in loads[2:]:
        load.wait()
    key = k_s[...]
    hidden = []
    for start in range(0, 512, step):
        rows = slice(start, start + step)
        gate = dot(wg_s[rows, :], key, NT)
        up = dot(wu_s[rows, :], key, NT)
        back = dot(down[rows], scaled, NN)
        sigma = jax.nn.sigmoid(gate)
        active = gate * sigma
        hidden.append((active * up).astype(BF16))
        grad_gate = (back * up * sigma * (1.0 + gate * (1.0 - sigma))).astype(BF16)
        grad_up = (back * active).astype(BF16)
        put(dot(grad_gate, key, NN).astype(BF16), 0, start)
        put(dot(grad_up, key, NN).astype(BF16), 1, start)
    ship(0, 0, 64, 64)
    hidden = jnp.concatenate(hidden, axis=0)
    for start in range(0, 512, step):
        rows = slice(start, start + step)
        put(dot(scaled[rows], hidden, NT).astype(BF16), 2, start)
    ship(1, 64, 96, 104)
    for store in stores:
        store.wait()


def grads(spot, k, v, rate, flag, wg, wu, wd):
    sm = pl.BlockSpec(memory_space=pltpu.SMEM)
    vm = pl.BlockSpec(memory_space=pltpu.VMEM)
    hb = pl.BlockSpec(memory_space=pltpu.HBM)
    return pl.pallas_call(
        grads_kernel,
        out_shape=(jax.ShapeDtypeStruct((8, 4, 104, 128), BF16),)
        + (jax.ShapeDtypeStruct((8, 96, 128), BF16),) * 4,
        in_specs=[sm] + [hb] * 5 + [vm, vm],
        out_specs=(hb,) * 5,
        scratch_shapes=[pltpu.VMEM((512, 512), BF16)] * 5
        + [
            pltpu.VMEM((4, 8, 104, 128), BF16),
            pltpu.VMEM((4, 8, 96, 128), BF16),
            pltpu.SemaphoreType.DMA((5,)),
            pltpu.SemaphoreType.DMA((2, 4)),
            pltpu.SemaphoreType.DMA((2, 4)),
        ],
        name="grads",
    )(spot, k, v, wg, wu, wd, rate, flag)


def fold_kernel(spot_ref, left_ref, own, one, two, three, right_hbm, *refs):
    lefts, (in_s, left_s, right_s, sem_in, sem_out) = refs[:4], refs[4:]
    layer_z = lax.rem(lax.div(spot_ref[0], 8), 4)
    loads = [
        pltpu.make_async_copy(src, in_s.at[i], sem_in.at[i])
        for i, src in enumerate((own, one, two, three))
    ]
    for load in loads:
        load.start()
    for z in range(4):
        left_s[z, :96, :] = jnp.sum(left_ref[:, z, :96, :].astype(F32), axis=0).astype(BF16)
    tail = jnp.sum(left_ref[:, 0, 96:104, :].astype(F32), axis=0)
    total = jnp.broadcast_to(tail[0:1] + tail[1:2], (8, 128))
    high = total.astype(BF16).astype(F32)
    row = lax.broadcasted_iota(jnp.int32, (8, 128), 0)
    tail = jnp.where(row == 0, high, jnp.where(row == 1, total - high, 0.0)).astype(BF16)
    left_s[:, 96:104, :] = jnp.broadcast_to(tail[None], (4, 8, 128))
    stores = [
        pltpu.make_async_copy(left_s.at[lax.rem(layer_z + d, 4)], lefts[d], sem_out.at[d])
        for d in range(4)
    ]
    for store in stores:
        store.start()
    for load in loads:
        load.wait()
    right_s[...] = jnp.sum(in_s[...].astype(F32), axis=0).astype(BF16)
    stores.append(pltpu.make_async_copy(right_s, right_hbm, sem_out.at[4]))
    stores[4].start()
    for store in stores:
        store.wait()


def fold(spot, left, rights):
    sm = pl.BlockSpec(memory_space=pltpu.SMEM)
    vm = pl.BlockSpec(memory_space=pltpu.VMEM)
    hb = pl.BlockSpec(memory_space=pltpu.HBM)
    return pl.pallas_call(
        fold_kernel,
        out_shape=(jax.ShapeDtypeStruct((8, 96, 128), BF16),)
        + (jax.ShapeDtypeStruct((104, 128), BF16),) * 4,
        in_specs=[sm, vm] + [hb] * 4,
        out_specs=(hb,) * 5,
        scratch_shapes=[
            pltpu.VMEM((4, 8, 96, 128), BF16),
            pltpu.VMEM((4, 104, 128), BF16),
            pltpu.VMEM((8, 96, 128), BF16),
            pltpu.SemaphoreType.DMA((4,)),
            pltpu.SemaphoreType.DMA((5,)),
        ],
        compiler_params=pltpu.CompilerParams(vmem_limit_bytes=FOLD_VMEM),
        name="fold",
    )(spot, left, *rights)


def renorm_kernel(
    spot_ref, right_ref, own, one, two, three, wg, wu, wd, left_hbm, right_hbm,
    in_s, old_s, left_s, right_s, sem_in, sem_w, sem_left, sem_right, *, update_len,
):
    rows = pl.ds(pl.multiple_of(lax.rem(spot_ref[0], 32) * 16, 16), 16)
    loads = [
        pltpu.make_async_copy(ref.at[0, rows], old_s.at[i], sem_w.at[i])
        for i, ref in enumerate((wg, wu, wd))
    ] + [
        pltpu.make_async_copy(src, in_s.at[i], sem_in.at[i])
        for i, src in enumerate((own, one, two, three))
    ]
    for load in loads:
        load.start()
    right = jnp.sum(right_ref[...].astype(F32), axis=0)
    for load in loads:
        load.wait()
    left = jnp.sum(in_s[...].astype(F32), axis=0)
    total = left[96:97, 0:1] + left[97:98, 0:1]
    factor = 2.0 * update_len / (total * math.sqrt(update_len * 512))
    for which in range(3):
        row = which * 32
        summed = jnp.concatenate(
            [half[row + c * 16 : row + c * 16 + 16] for half in (left, right) for c in range(2)], axis=1
        )
        old = old_s[which].astype(F32)
        updated = old + summed * factor
        old_norm = jnp.sqrt(jnp.sum(old * old, axis=-1, keepdims=True))
        new_norm = jnp.sqrt(jnp.sum(updated * updated, axis=-1, keepdims=True) + 1e-6)
        fresh = (updated * (old_norm / new_norm)).astype(BF16)
        left_s[which] = fresh[:, :256]
        right_s[which] = fresh[:, 256:]
    stores = [pltpu.make_async_copy(right_s, right_hbm.at[d], sem_right.at[d]) for d in range(16)]
    stores.append(pltpu.make_async_copy(left_s, left_hbm, sem_left))
    for store in stores:
        store.start()
    for store in stores:
        store.wait()


def renorm(spot, right, lefts, wg, wu, wd, update_len):
    sm = pl.BlockSpec(memory_space=pltpu.SMEM)
    vm = pl.BlockSpec(memory_space=pltpu.VMEM)
    hb = pl.BlockSpec(memory_space=pltpu.HBM)
    return pl.pallas_call(
        functools.partial(renorm_kernel, update_len=update_len),
        out_shape=(
            jax.ShapeDtypeStruct((3, 16, 256), BF16),
            jax.ShapeDtypeStruct((16, 3, 16, 256), BF16),
        ),
        in_specs=[sm, vm] + [hb] * 7,
        out_specs=(hb, hb),
        scratch_shapes=[
            pltpu.VMEM((4, 104, 128), BF16),
            pltpu.VMEM((3, 16, 512), BF16),
            pltpu.VMEM((3, 16, 256), BF16),
            pltpu.VMEM((3, 16, 256), BF16),
            pltpu.SemaphoreType.DMA((4,)),
            pltpu.SemaphoreType.DMA((3,)),
            pltpu.SemaphoreType.DMA,
            pltpu.SemaphoreType.DMA((16,)),
        ],
        compiler_params=pltpu.CompilerParams(vmem_limit_bytes=RENORM_VMEM),
        name="renorm",
    )(spot, right, *lefts, wg, wu, wd)


def attend_kernel(
    pos_ref, doc_ref, q_hbm, k_hbm, v_hbm, pk_hbm, pv_hbm, out_hbm,
    q_ref, k_ref, v_ref, pk_ref, pv_ref, att_s, sem,
):
    base = pos_ref[0] * 512
    loads = [
        pltpu.make_async_copy(src.at[0], dst, sem.at[i])
        for i, (src, dst) in enumerate(
            (
                (q_hbm, q_ref),
                (k_hbm, k_ref),
                (v_hbm, v_ref),
                (pk_hbm, pk_ref),
                (pv_hbm, pv_ref),
            )
        )
    ]
    for load in loads:
        load.start()

    for load in loads:
        load.wait()
    step = 128
    scale = 1.0 / math.sqrt(512)
    doc = (jnp.broadcast_to(doc_ref[...], (8, 512)) - base).T[:, :1]
    for start in range(0, 512, step):
        rows = slice(start, start + step)
        q = q_ref[rows, :]
        keys = jnp.concatenate([pk_ref[start:, :], k_ref[: start + step, :]], axis=0)
        vals = jnp.concatenate([pv_ref[start:, :], v_ref[: start + step, :]], axis=0)
        width = 512 + step
        s = dot(q, keys, NT) * scale
        at = lax.broadcasted_iota(jnp.int32, (step, width), 0) + start
        to = lax.broadcasted_iota(jnp.int32, (step, width), 1) + (start - 512)
        ok = (to <= at) & (to > at - 512) & (to >= doc[rows])
        s = jnp.where(ok, s, -1e30)
        top = jnp.max(s, axis=-1, keepdims=True)
        e = jnp.exp(s - top)
        prob = (e / jnp.sum(e, axis=-1, keepdims=True)).astype(BF16)
        att_s[rows, :] = dot(prob, vals, NN)
    store = pltpu.make_async_copy(att_s, out_hbm.at[0], sem.at[5])
    store.start()
    store.wait()


def attend(pos, q, k, v, doc, pk, pv):
    vm = pl.BlockSpec(memory_space=pltpu.VMEM)
    hb = pl.BlockSpec(memory_space=pltpu.HBM)
    return pl.pallas_call(
        attend_kernel,
        out_shape=jax.ShapeDtypeStruct((2, 512, 512), F32),
        in_specs=[pl.BlockSpec(memory_space=pltpu.SMEM), vm] + [hb] * 5,
        out_specs=hb,
        scratch_shapes=[pltpu.VMEM((512, 512), BF16)] * 5
        + [
            pltpu.VMEM((512, 512), F32),
            pltpu.SemaphoreType.DMA((6,)),
        ],
        name="attend",
    )(pos, doc, q, k, v, pk, pv)


def relay_kernel(
    spot_ref, right, zero, one, two, three, wg, wu, wd, left_hbm, right_hbm,
    left_s, right_s, sem_in, sem_out, sem_right,
):
    first = spot_ref[0] < 32
    layer_z = lax.rem(lax.div(spot_ref[0], 8), 4)
    column = lax.rem(spot_ref[0], 8)

    def send(source):
        store = pltpu.make_async_copy(source, right_hbm, sem_right)
        store.start()
        copies = [pltpu.make_async_copy(left_s, left_hbm.at[d], sem_out.at[d]) for d in range(8)]
        for copy in copies:
            copy.start()
        for copy in copies:
            copy.wait()
        store.wait()

    @pl.when(first)
    def _():
        copies = []
        for i, ref in enumerate((wg, wu, wd)):
            copies.append(
                pltpu.make_async_copy(ref.at[:, column, :, pl.ds(0, 256)], left_s.at[:, i], sem_in.at[i])
            )
            copies.append(
                pltpu.make_async_copy(
                    ref.at[layer_z, :, :, pl.ds(256, 256)], right_s.at[:, i], sem_in.at[i + 3]
                )
            )
        for copy in copies:
            copy.start()
        for copy in copies:
            copy.wait()
        send(right_s)

    @pl.when(jnp.logical_not(first))
    def _():
        copies = [
            pltpu.make_async_copy(src, left_s.at[lax.rem(layer_z + 4 - d, 4)], sem_in.at[d])
            for d, src in enumerate((zero, one, two, three))
        ]
        for copy in copies:
            copy.start()
        for copy in copies:
            copy.wait()
        send(right.at[pl.ds(0, 8)])


def relay(spot, right, lefts, wg, wu, wd):
    sm = pl.BlockSpec(memory_space=pltpu.SMEM)
    vm = pl.BlockSpec(memory_space=pltpu.VMEM)
    hb = pl.BlockSpec(memory_space=pltpu.HBM)
    return pl.pallas_call(
        relay_kernel,
        out_shape=(
            jax.ShapeDtypeStruct((8, 4, 3, 16, 256), BF16),
            jax.ShapeDtypeStruct((8, 3, 16, 256), BF16),
        ),
        in_specs=[sm, vm] + [hb] * 7,
        out_specs=(hb, hb),
        scratch_shapes=[
            pltpu.VMEM((4, 3, 16, 256), BF16),
            pltpu.VMEM((8, 3, 16, 256), BF16),
            pltpu.SemaphoreType.DMA((6,)),
            pltpu.SemaphoreType.DMA((8,)),
            pltpu.SemaphoreType.DMA,
        ],
        compiler_params=pltpu.CompilerParams(vmem_limit_bytes=RELAY_VMEM),
        name="relay",
    )(spot, right, *lefts, *(x.reshape(4, 8, 16, 512) for x in (wg, wu, wd)))


def apply_kernel(
    spot_ref, left, own, one, two, three, q_hbm, att_hbm, wc_hbm, mixed_hbm, part_hbm,
    right, q_s, att_s, wc_s, mixed_s, part_s, sem_in, sem_right, sem_out,
):
    layer_z = lax.rem(lax.div(spot_ref[0], 8), 4)
    slabs = [
        pltpu.make_async_copy(src, right.at[lax.rem(layer_z + 4 - d, 4)], sem_right.at[d])
        for d, src in enumerate((own, one, two, three))
    ]
    for slab in slabs:
        slab.start()
    loads = [
        pltpu.make_async_copy(src, dst, sem_in.at[i])
        for i, (src, dst) in enumerate(((q_hbm.at[0], q_s), (att_hbm.at[0], att_s), (wc_hbm, wc_s)))
    ]
    for load in loads:
        load.start()

    def weight(i, low, count):
        spots = [(z, y) for z in range(low // 128, (low + count) // 128) for y in range(8)]
        return jnp.concatenate(
            [
                jnp.concatenate([left[y, z, i] for z, y in spots], axis=0),
                jnp.concatenate([right[z, y, i] for z, y in spots], axis=0),
            ],
            axis=1,
        )

    step = APPLY_STEP
    loads[0].wait()
    for slab in slabs:
        slab.wait()
    q = q_s[...]
    hidden = []
    for start in range(0, 512, step):
        gate = dot(q, weight(0, start, step), NT)
        up = dot(q, weight(1, start, step), NT)
        hidden.append((gate * jax.nn.sigmoid(gate) * up).astype(BF16))
    hidden = jnp.concatenate(hidden, axis=1)
    loads[1].wait()
    for start in range(0, 512, step):
        cols = slice(start, start + step)
        mixed_s[:, cols] = (att_s[:, cols] + dot(hidden, weight(2, start, step), NT)).astype(BF16)
    stores = [pltpu.make_async_copy(mixed_s, mixed_hbm.at[0], sem_out.at[0])]
    stores[0].start()
    loads[2].wait()
    mixed = mixed_s[...]
    for start in range(0, 512, step):
        cols = slice(start, start + step)
        part_s[:, cols] = dot(mixed, wc_s[:, cols], NN).astype(BF16)
    stores.append(pltpu.make_async_copy(part_s, part_hbm, sem_out.at[1]))
    stores[1].start()
    for store in stores:
        store.wait()


def fast_apply(spot, left, rights, q, att, wc):
    vm = pl.BlockSpec(memory_space=pltpu.VMEM)
    hb = pl.BlockSpec(memory_space=pltpu.HBM)
    return pl.pallas_call(
        apply_kernel,
        out_shape=(
            jax.ShapeDtypeStruct((1, 512, 512), BF16),
            jax.ShapeDtypeStruct((512, 512), BF16),
        ),
        in_specs=[pl.BlockSpec(memory_space=pltpu.SMEM), vm] + [hb] * 7,
        out_specs=(hb, hb),
        scratch_shapes=[
            pltpu.VMEM((4, 8, 3, 16, 256), BF16),
            pltpu.VMEM((512, 512), BF16),
            pltpu.VMEM((512, 512), F32),
            pltpu.VMEM((512, 512), BF16),
            pltpu.VMEM((512, 512), BF16),
            pltpu.VMEM((512, 512), BF16),
            pltpu.SemaphoreType.DMA((3,)),
            pltpu.SemaphoreType.DMA((4,)),
            pltpu.SemaphoreType.DMA((2,)),
        ],
        compiler_params=pltpu.CompilerParams(vmem_limit_bytes=APPLY_VMEM),
        name="fast_apply",
    )(spot, left, *rights, q, att, wc)


def combine_kernel(recv_ref, flag_ref, out_ref):
    summed = jnp.sum(recv_ref[...].astype(F32), axis=0)
    flag = jnp.broadcast_to(flag_ref[...].astype(F32), (8, 64)).T[:, :1]
    out_ref[0] = (summed * flag).astype(BF16)


def combine(recv, flag):
    vm = pl.BlockSpec(memory_space=pltpu.VMEM)
    return pl.pallas_call(
        combine_kernel,
        out_shape=jax.ShapeDtypeStruct((1, 64, 512), BF16),
        in_specs=[vm, vm],
        out_specs=vm,
        compiler_params=pltpu.CompilerParams(vmem_limit_bytes=4 << 20),
        name="combine",
    )(recv, flag)


def layer(q, k, v, rate, doc_start, flag, wg, wu, wd, wc):
    seq_count = lax.axis_size("seq")
    half = seq_count // 2
    index = lax.axis_index("seq").astype(jnp.int32)
    place = lambda z, y: z * 8 + y
    slabs = [[place(z + lift, y) for lift in (0, 4) for y in range(8)] for z in range(4)]
    rows = [[place(z, y) for y in range(8)] for z in range(8)]
    route = [(i - 1, i) for i in range(1, seq_count)]

    def turn(block, d):
        pairs = [
            (place(z + lift, y), place((z + d) % 4 + lift, y))
            for lift in (0, 4)
            for z in range(4)
            for y in range(8)
        ]
        return lax.ppermute(block, "seq", pairs)

    def lift_up(block, d):
        pairs = [(place(z, y), place((z + d) % 4 + 4, y)) for z in range(4) for y in range(8)]
        return lax.ppermute(block, "seq", pairs)

    spot = index[None]
    pk = lax.ppermute(k, "seq", route)
    pv = lax.ppermute(v, "seq", route)
    left, *rights = grads(spot, k, v, rate, flag[None], wg, wu, wd)
    left = lax.all_to_all(left, "seq", 0, 0, axis_index_groups=rows)
    rights = [rights[0]] + [turn(rights[d], d) for d in range(1, 4)]
    right, *lefts = fold(spot, left, rights)
    right = lax.all_to_all(right, "seq", 0, 0, axis_index_groups=rows)
    lefts = [lefts[0]] + [turn(lefts[d], d) for d in range(1, 4)]
    left, right = renorm(spot, right, lefts, wg, wu, wd, 512 * half)
    right = lax.all_to_all(right, "seq", 0, 0, axis_index_groups=slabs)
    lefts = [lift_up(left, d) for d in range(4)]
    left, right = relay(spot, right, lefts, wg, wu, wd)
    left = lax.all_to_all(left, "seq", 0, 0, axis_index_groups=rows)
    rights = [right] + [turn(right, d) for d in range(1, 4)]
    att = attend(spot, q, k, v, doc_start[None], pk, pv)
    mixed, part = fast_apply(spot, left, rights, q, att, wc)
    flags = lax.dynamic_slice_in_dim(flag, lax.axis_index("head") * 64, 64, 0)[None]
    got = lax.all_to_all(part.reshape(8, 64, 512), "head", 0, 0)
    return mixed, combine(got, flags)


def solution(mesh):
    placed = (
        P("head", "seq", None),
        P("head", "seq", None),
        P("head", "seq", None),
        P("head", "seq"),
        P("seq"),
        P("seq"),
        P("head", None, None),
        P("head", None, None),
        P("head", None, None),
        P("head", None),
    )
    return jax.shard_map(
        layer,
        mesh=mesh,
        in_specs=placed,
        out_specs=(P("head", "seq", None), P("seq", "head", None)),
        check_vma=False,
    )
```

```python
import functools
import math
import jax
import jax.numpy as jnp
from jax import lax
from jax.experimental import pallas as pl
from jax.experimental.pallas import tpu as pltpu
from jax.sharding import PartitionSpec as P


F32 = jnp.float32
GRADS_STEP = 256
APPLY_STEP = 256
FOLD_VMEM = 53000 << 10
RENORM_VMEM = 53000 << 10
RELAY_VMEM = 53000 << 10
APPLY_VMEM = 50800 << 10
BF16 = jnp.bfloat16
NN = (((1,), (0,)), ((), ()))
NT = (((1,), (1,)), ((), ()))


def dot(a, b, dims):
    return lax.dot_general(a, b, dims, preferred_element_type=F32)


def grads_kernel(
    spot_ref, k_hbm, v_hbm, wg_hbm, wu_hbm, wd_hbm, rate_ref, flag_ref, left_hbm, kv_hbm, *refs
):
    rights, (k_s, v_s, wg_s, wu_s, wd_s, left_s, right_s, *sems) = refs[:4], refs[4:]
    sem_in, sem_left, sem_right, sem_kv = sems
    layer_z = lax.rem(lax.div(spot_ref[0], 8), 4)
    loads = [
        pltpu.make_async_copy(src.at[0], dst, sem_in.at[i])
        for i, (src, dst) in enumerate(
            ((v_hbm, v_s), (wd_hbm, wd_s), (k_hbm, k_s), (wg_hbm, wg_s), (wu_hbm, wu_s))
        )
    ]
    for load in loads:
        load.start()
    step = GRADS_STEP
    stores = []

    def put(piece, which, start):
        for n in range(step // 16):
            z, y = divmod(start // 16 + n, 8)
            for c in range(4):
                block = piece[n * 16 : n * 16 + 16, c * 128 : (c + 1) * 128]
                row = which * 32 + (c % 2) * 16
                (left_s, right_s)[c // 2][z, y, row : row + 16, :] = block

    def ship(phase, low, high, top):
        for z in range(4):
            store = pltpu.make_async_copy(
                left_s.at[z, :, low:top], left_hbm.at[:, z, low:top], sem_left.at[phase, z]
            )
            store.start()
            stores.append(store)
        for d in range(4):
            store = pltpu.make_async_copy(
                right_s.at[lax.rem(layer_z + d, 4), :, low:high],
                rights[d].at[:, low:high],
                sem_right.at[phase, d],
            )
            store.start()
            stores.append(store)

    rate = rate_ref[...]
    coeff = flag_ref[...].astype(F32) * rate
    total = jnp.sum(rate, axis=1, keepdims=True)
    high = total.astype(BF16)
    low = (total - high.astype(F32)).astype(BF16)
    row = lax.broadcasted_iota(jnp.int32, (8, 128), 0)
    tail = jnp.where(row == 0, high.astype(F32), jnp.where(row == 1, low.astype(F32), 0.0))
    left_s[:, :, 96:104, :] = jnp.broadcast_to(tail.astype(BF16)[None, None], (4, 8, 8, 128))
    loads[0].wait()
    scaled = (coeff * v_s[...].T.astype(F32)).astype(BF16)
    loads[1].wait()
    down = wd_s[...].T
    for load in loads[2:]:
        load.wait()
    for i, src in enumerate((k_s, v_s)):
        stores.append(pltpu.make_async_copy(src, kv_hbm.at[i], sem_kv.at[i]))
        stores[i].start()
    key = k_s[...]
    hidden = []
    for start in range(0, 512, step):
        rows = slice(start, start + step)
        gate = dot(wg_s[rows, :], key, NT)
        up = dot(wu_s[rows, :], key, NT)
        back = dot(down[rows], scaled, NN)
        sigma = jax.nn.sigmoid(gate)
        active = gate * sigma
        hidden.append((active * up).astype(BF16))
        grad_gate = (back * up * sigma * (1.0 + gate * (1.0 - sigma))).astype(BF16)
        grad_up = (back * active).astype(BF16)
        put(dot(grad_gate, key, NN).astype(BF16), 0, start)
        put(dot(grad_up, key, NN).astype(BF16), 1, start)
    ship(0, 0, 64, 64)
    hidden = jnp.concatenate(hidden, axis=0)
    for start in range(0, 512, step):
        rows = slice(start, start + step)
        put(dot(scaled[rows], hidden, NT).astype(BF16), 2, start)
    ship(1, 64, 96, 104)
    for store in stores:
        store.wait()


def grads(spot, k, v, rate, flag, wg, wu, wd):
    sm = pl.BlockSpec(memory_space=pltpu.SMEM)
    vm = pl.BlockSpec(memory_space=pltpu.VMEM)
    hb = pl.BlockSpec(memory_space=pltpu.HBM)
    return pl.pallas_call(
        grads_kernel,
        out_shape=(
            jax.ShapeDtypeStruct((8, 4, 104, 128), BF16),
            jax.ShapeDtypeStruct((2, 512, 512), BF16),
        )
        + (jax.ShapeDtypeStruct((8, 96, 128), BF16),) * 4,
        in_specs=[sm] + [hb] * 5 + [vm, vm],
        out_specs=(hb,) * 6,
        scratch_shapes=[pltpu.VMEM((512, 512), BF16)] * 5
        + [
            pltpu.VMEM((4, 8, 104, 128), BF16),
            pltpu.VMEM((4, 8, 96, 128), BF16),
            pltpu.SemaphoreType.DMA((5,)),
            pltpu.SemaphoreType.DMA((2, 4)),
            pltpu.SemaphoreType.DMA((2, 4)),
            pltpu.SemaphoreType.DMA((2,)),
        ],
        name="grads",
    )(spot, k, v, wg, wu, wd, rate, flag)


def fold_kernel(spot_ref, left_ref, own, one, two, three, right_hbm, *refs):
    lefts, (in_s, left_s, right_s, sem_in, sem_out) = refs[:4], refs[4:]
    layer_z = lax.rem(lax.div(spot_ref[0], 8), 4)
    loads = [
        pltpu.make_async_copy(src, in_s.at[i], sem_in.at[i])
        for i, src in enumerate((own, one, two, three))
    ]
    for load in loads:
        load.start()
    for z in range(4):
        left_s[z, :96, :] = jnp.sum(left_ref[:, z, :96, :].astype(F32), axis=0).astype(BF16)
    tail = jnp.sum(left_ref[:, 0, 96:104, :].astype(F32), axis=0)
    total = jnp.broadcast_to(tail[0:1] + tail[1:2], (8, 128))
    high = total.astype(BF16).astype(F32)
    row = lax.broadcasted_iota(jnp.int32, (8, 128), 0)
    tail = jnp.where(row == 0, high, jnp.where(row == 1, total - high, 0.0)).astype(BF16)
    left_s[:, 96:104, :] = jnp.broadcast_to(tail[None], (4, 8, 128))
    stores = [
        pltpu.make_async_copy(left_s.at[lax.rem(layer_z + d, 4)], lefts[d], sem_out.at[d])
        for d in range(4)
    ]
    for store in stores:
        store.start()
    for load in loads:
        load.wait()
    right_s[...] = jnp.sum(in_s[...].astype(F32), axis=0).astype(BF16)
    stores.append(pltpu.make_async_copy(right_s, right_hbm, sem_out.at[4]))
    stores[4].start()
    for store in stores:
        store.wait()


def fold(spot, left, rights):
    sm = pl.BlockSpec(memory_space=pltpu.SMEM)
    vm = pl.BlockSpec(memory_space=pltpu.VMEM)
    hb = pl.BlockSpec(memory_space=pltpu.HBM)
    return pl.pallas_call(
        fold_kernel,
        out_shape=(jax.ShapeDtypeStruct((8, 96, 128), BF16),)
        + (jax.ShapeDtypeStruct((104, 128), BF16),) * 4,
        in_specs=[sm, vm] + [hb] * 4,
        out_specs=(hb,) * 5,
        scratch_shapes=[
            pltpu.VMEM((4, 8, 96, 128), BF16),
            pltpu.VMEM((4, 104, 128), BF16),
            pltpu.VMEM((8, 96, 128), BF16),
            pltpu.SemaphoreType.DMA((4,)),
            pltpu.SemaphoreType.DMA((5,)),
        ],
        compiler_params=pltpu.CompilerParams(vmem_limit_bytes=FOLD_VMEM),
        name="fold",
    )(spot, left, *rights)


def renorm_kernel(
    spot_ref, right_ref, own, one, two, three, wg, wu, wd, left_hbm, right_hbm,
    in_s, old_s, left_s, right_s, sem_in, sem_w, sem_left, sem_right, *, update_len,
):
    rows = pl.ds(pl.multiple_of(lax.rem(spot_ref[0], 32) * 16, 16), 16)
    loads = [
        pltpu.make_async_copy(ref.at[0, rows], old_s.at[i], sem_w.at[i])
        for i, ref in enumerate((wg, wu, wd))
    ] + [
        pltpu.make_async_copy(src, in_s.at[i], sem_in.at[i])
        for i, src in enumerate((own, one, two, three))
    ]
    for load in loads:
        load.start()
    right = jnp.sum(right_ref[...].astype(F32), axis=0)
    for load in loads:
        load.wait()
    left = jnp.sum(in_s[...].astype(F32), axis=0)
    total = left[96:97, 0:1] + left[97:98, 0:1]
    factor = 2.0 * update_len / (total * math.sqrt(update_len * 512))
    for which in range(3):
        row = which * 32
        summed = jnp.concatenate(
            [half[row + c * 16 : row + c * 16 + 16] for half in (left, right) for c in range(2)], axis=1
        )
        old = old_s[which].astype(F32)
        updated = old + summed * factor
        old_norm = jnp.sqrt(jnp.sum(old * old, axis=-1, keepdims=True))
        new_norm = jnp.sqrt(jnp.sum(updated * updated, axis=-1, keepdims=True) + 1e-6)
        fresh = (updated * (old_norm / new_norm)).astype(BF16)
        left_s[which] = fresh[:, :256]
        right_s[which] = fresh[:, 256:]
    stores = [pltpu.make_async_copy(right_s, right_hbm.at[d], sem_right.at[d]) for d in range(16)]
    stores.append(pltpu.make_async_copy(left_s, left_hbm, sem_left))
    for store in stores:
        store.start()
    for store in stores:
        store.wait()


def renorm(spot, right, lefts, wg, wu, wd, update_len):
    sm = pl.BlockSpec(memory_space=pltpu.SMEM)
    vm = pl.BlockSpec(memory_space=pltpu.VMEM)
    hb = pl.BlockSpec(memory_space=pltpu.HBM)
    return pl.pallas_call(
        functools.partial(renorm_kernel, update_len=update_len),
        out_shape=(
            jax.ShapeDtypeStruct((3, 16, 256), BF16),
            jax.ShapeDtypeStruct((16, 3, 16, 256), BF16),
        ),
        in_specs=[sm, vm] + [hb] * 7,
        out_specs=(hb, hb),
        scratch_shapes=[
            pltpu.VMEM((4, 104, 128), BF16),
            pltpu.VMEM((3, 16, 512), BF16),
            pltpu.VMEM((3, 16, 256), BF16),
            pltpu.VMEM((3, 16, 256), BF16),
            pltpu.SemaphoreType.DMA((4,)),
            pltpu.SemaphoreType.DMA((3,)),
            pltpu.SemaphoreType.DMA,
            pltpu.SemaphoreType.DMA((16,)),
        ],
        compiler_params=pltpu.CompilerParams(vmem_limit_bytes=RENORM_VMEM),
        name="renorm",
    )(spot, right, *lefts, wg, wu, wd)


def attend_kernel(
    pos_ref, doc_ref, q_hbm, k_hbm, v_hbm, prev_hbm, out_hbm,
    q_ref, k_ref, v_ref, pk_ref, pv_ref, att_s, sem,
):
    base = pos_ref[0] * 512
    loads = [
        pltpu.make_async_copy(src.at[n], dst, sem.at[i])
        for i, (src, dst, n) in enumerate(
            (
                (q_hbm, q_ref, 0),
                (k_hbm, k_ref, 0),
                (v_hbm, v_ref, 0),
                (prev_hbm, pk_ref, 0),
                (prev_hbm, pv_ref, 1),
            )
        )
    ]
    for load in loads:
        load.start()

    for load in loads:
        load.wait()
    step = 128
    scale = 1.0 / math.sqrt(512)
    doc = (jnp.broadcast_to(doc_ref[...], (8, 512)) - base).T[:, :1]
    for start in range(0, 512, step):
        rows = slice(start, start + step)
        q = q_ref[rows, :]
        keys = jnp.concatenate([pk_ref[start:, :], k_ref[: start + step, :]], axis=0)
        vals = jnp.concatenate([pv_ref[start:, :], v_ref[: start + step, :]], axis=0)
        width = 512 + step
        s = dot(q, keys, NT) * scale
        at = lax.broadcasted_iota(jnp.int32, (step, width), 0) + start
        to = lax.broadcasted_iota(jnp.int32, (step, width), 1) + (start - 512)
        ok = (to <= at) & (to > at - 512) & (to >= doc[rows])
        s = jnp.where(ok, s, -1e30)
        top = jnp.max(s, axis=-1, keepdims=True)
        e = jnp.exp(s - top)
        prob = (e / jnp.sum(e, axis=-1, keepdims=True)).astype(BF16)
        att_s[rows, :] = dot(prob, vals, NN)
    store = pltpu.make_async_copy(att_s, out_hbm.at[0], sem.at[5])
    store.start()
    store.wait()


def attend(pos, q, k, v, doc, prev):
    vm = pl.BlockSpec(memory_space=pltpu.VMEM)
    hb = pl.BlockSpec(memory_space=pltpu.HBM)
    return pl.pallas_call(
        attend_kernel,
        out_shape=jax.ShapeDtypeStruct((2, 512, 512), F32),
        in_specs=[pl.BlockSpec(memory_space=pltpu.SMEM), vm] + [hb] * 4,
        out_specs=hb,
        scratch_shapes=[pltpu.VMEM((512, 512), BF16)] * 5
        + [
            pltpu.VMEM((512, 512), F32),
            pltpu.SemaphoreType.DMA((6,)),
        ],
        name="attend",
    )(pos, doc, q, k, v, prev)


def relay_kernel(
    spot_ref, right, zero, one, two, three, wg, wu, wd, left_hbm, right_hbm,
    left_s, right_s, sem_in, sem_out, sem_right,
):
    first = spot_ref[0] < 32
    layer_z = lax.rem(lax.div(spot_ref[0], 8), 4)
    column = lax.rem(spot_ref[0], 8)

    def send(source):
        store = pltpu.make_async_copy(source, right_hbm, sem_right)
        store.start()
        copies = [pltpu.make_async_copy(left_s, left_hbm.at[d], sem_out.at[d]) for d in range(8)]
        for copy in copies:
            copy.start()
        for copy in copies:
            copy.wait()
        store.wait()

    @pl.when(first)
    def _():
        copies = []
        for i, ref in enumerate((wg, wu, wd)):
            copies.append(
                pltpu.make_async_copy(ref.at[:, column, :, pl.ds(0, 256)], left_s.at[:, i], sem_in.at[i])
            )
            copies.append(
                pltpu.make_async_copy(
                    ref.at[layer_z, :, :, pl.ds(256, 256)], right_s.at[:, i], sem_in.at[i + 3]
                )
            )
        for copy in copies:
            copy.start()
        for copy in copies:
            copy.wait()
        send(right_s)

    @pl.when(jnp.logical_not(first))
    def _():
        copies = [
            pltpu.make_async_copy(src, left_s.at[lax.rem(layer_z + 4 - d, 4)], sem_in.at[d])
            for d, src in enumerate((zero, one, two, three))
        ]
        for copy in copies:
            copy.start()
        for copy in copies:
            copy.wait()
        send(right.at[pl.ds(0, 8)])


def relay(spot, right, lefts, wg, wu, wd):
    sm = pl.BlockSpec(memory_space=pltpu.SMEM)
    vm = pl.BlockSpec(memory_space=pltpu.VMEM)
    hb = pl.BlockSpec(memory_space=pltpu.HBM)
    return pl.pallas_call(
        relay_kernel,
        out_shape=(
            jax.ShapeDtypeStruct((8, 4, 3, 16, 256), BF16),
            jax.ShapeDtypeStruct((8, 3, 16, 256), BF16),
        ),
        in_specs=[sm, vm] + [hb] * 7,
        out_specs=(hb, hb),
        scratch_shapes=[
            pltpu.VMEM((4, 3, 16, 256), BF16),
            pltpu.VMEM((8, 3, 16, 256), BF16),
            pltpu.SemaphoreType.DMA((6,)),
            pltpu.SemaphoreType.DMA((8,)),
            pltpu.SemaphoreType.DMA,
        ],
        compiler_params=pltpu.CompilerParams(vmem_limit_bytes=RELAY_VMEM),
        name="relay",
    )(spot, right, *lefts, *(x.reshape(4, 8, 16, 512) for x in (wg, wu, wd)))


def apply_kernel(
    spot_ref, left, own, one, two, three, q_hbm, att_hbm, wc_hbm, mixed_hbm, part_hbm,
    right, q_s, att_s, wc_s, mixed_s, part_s, sem_in, sem_right, sem_out,
):
    layer_z = lax.rem(lax.div(spot_ref[0], 8), 4)
    slabs = [
        pltpu.make_async_copy(src, right.at[lax.rem(layer_z + 4 - d, 4)], sem_right.at[d])
        for d, src in enumerate((own, one, two, three))
    ]
    for slab in slabs:
        slab.start()
    loads = [
        pltpu.make_async_copy(src, dst, sem_in.at[i])
        for i, (src, dst) in enumerate(((q_hbm.at[0], q_s), (att_hbm.at[0], att_s), (wc_hbm, wc_s)))
    ]
    for load in loads:
        load.start()

    def weight(i, low, count):
        spots = [(z, y) for z in range(low // 128, (low + count) // 128) for y in range(8)]
        return jnp.concatenate(
            [
                jnp.concatenate([left[y, z, i] for z, y in spots], axis=0),
                jnp.concatenate([right[z, y, i] for z, y in spots], axis=0),
            ],
            axis=1,
        )

    step = APPLY_STEP
    loads[0].wait()
    for slab in slabs:
        slab.wait()
    q = q_s[...]
    hidden = []
    for start in range(0, 512, step):
        gate = dot(q, weight(0, start, step), NT)
        up = dot(q, weight(1, start, step), NT)
        hidden.append((gate * jax.nn.sigmoid(gate) * up).astype(BF16))
    hidden = jnp.concatenate(hidden, axis=1)
    loads[1].wait()
    for start in range(0, 512, step):
        cols = slice(start, start + step)
        mixed_s[:, cols] = (att_s[:, cols] + dot(hidden, weight(2, start, step), NT)).astype(BF16)
    stores = [pltpu.make_async_copy(mixed_s, mixed_hbm.at[0], sem_out.at[0])]
    stores[0].start()
    loads[2].wait()
    mixed = mixed_s[...]
    for start in range(0, 512, step):
        cols = slice(start, start + step)
        part_s[:, cols] = dot(mixed, wc_s[:, cols], NN).astype(BF16)
    stores.append(pltpu.make_async_copy(part_s, part_hbm, sem_out.at[1]))
    stores[1].start()
    for store in stores:
        store.wait()


def fast_apply(spot, left, rights, q, att, wc):
    vm = pl.BlockSpec(memory_space=pltpu.VMEM)
    hb = pl.BlockSpec(memory_space=pltpu.HBM)
    return pl.pallas_call(
        apply_kernel,
        out_shape=(
            jax.ShapeDtypeStruct((1, 512, 512), BF16),
            jax.ShapeDtypeStruct((512, 512), BF16),
        ),
        in_specs=[pl.BlockSpec(memory_space=pltpu.SMEM), vm] + [hb] * 7,
        out_specs=(hb, hb),
        scratch_shapes=[
            pltpu.VMEM((4, 8, 3, 16, 256), BF16),
            pltpu.VMEM((512, 512), BF16),
            pltpu.VMEM((512, 512), F32),
            pltpu.VMEM((512, 512), BF16),
            pltpu.VMEM((512, 512), BF16),
            pltpu.VMEM((512, 512), BF16),
            pltpu.SemaphoreType.DMA((3,)),
            pltpu.SemaphoreType.DMA((4,)),
            pltpu.SemaphoreType.DMA((2,)),
        ],
        compiler_params=pltpu.CompilerParams(vmem_limit_bytes=APPLY_VMEM),
        name="fast_apply",
    )(spot, left, *rights, q, att, wc)


def combine_kernel(recv_ref, flag_ref, out_ref):
    summed = jnp.sum(recv_ref[...].astype(F32), axis=0)
    flag = jnp.broadcast_to(flag_ref[...].astype(F32), (8, 64)).T[:, :1]
    out_ref[0] = (summed * flag).astype(BF16)


def combine(recv, flag):
    vm = pl.BlockSpec(memory_space=pltpu.VMEM)
    return pl.pallas_call(
        combine_kernel,
        out_shape=jax.ShapeDtypeStruct((1, 64, 512), BF16),
        in_specs=[vm, vm],
        out_specs=vm,
        compiler_params=pltpu.CompilerParams(vmem_limit_bytes=4 << 20),
        name="combine",
    )(recv, flag)


def layer(q, k, v, rate, doc_start, flag, wg, wu, wd, wc):
    seq_count = lax.axis_size("seq")
    half = seq_count // 2
    index = lax.axis_index("seq").astype(jnp.int32)
    place = lambda z, y: z * 8 + y
    slabs = [[place(z + lift, y) for lift in (0, 4) for y in range(8)] for z in range(4)]
    rows = [[place(z, y) for y in range(8)] for z in range(8)]
    route = [(i - 1, i) for i in range(1, seq_count)]

    def turn(block, d):
        pairs = [
            (place(z + lift, y), place((z + d) % 4 + lift, y))
            for lift in (0, 4)
            for z in range(4)
            for y in range(8)
        ]
        return lax.ppermute(block, "seq", pairs)

    def lift_up(block, d):
        pairs = [(place(z, y), place((z + d) % 4 + 4, y)) for z in range(4) for y in range(8)]
        return lax.ppermute(block, "seq", pairs)

    spot = index[None]
    left, kv, *rights = grads(spot, k, v, rate, flag[None], wg, wu, wd)
    left = lax.all_to_all(left, "seq", 0, 0, axis_index_groups=rows)
    rights = [rights[0]] + [turn(rights[d], d) for d in range(1, 4)]
    right, *lefts = fold(spot, left, rights)
    right = lax.all_to_all(right, "seq", 0, 0, axis_index_groups=rows)
    lefts = [lefts[0]] + [turn(lefts[d], d) for d in range(1, 4)]
    prev = lax.ppermute(kv, "seq", route)
    left, right = renorm(spot, right, lefts, wg, wu, wd, 512 * half)
    right = lax.all_to_all(right, "seq", 0, 0, axis_index_groups=slabs)
    lefts = [lift_up(left, d) for d in range(4)]
    left, right = relay(spot, right, lefts, wg, wu, wd)
    left = lax.all_to_all(left, "seq", 0, 0, axis_index_groups=rows)
    rights = [right] + [turn(right, d) for d in range(1, 4)]
    att = attend(spot, q, k, v, doc_start[None], prev)
    mixed, part = fast_apply(spot, left, rights, q, att, wc)
    flags = lax.dynamic_slice_in_dim(flag, lax.axis_index("head") * 64, 64, 0)[None]
    got = lax.all_to_all(part.reshape(8, 64, 512), "head", 0, 0)
    return mixed, combine(got, flags)


def solution(mesh):
    placed = (
        P("head", "seq", None),
        P("head", "seq", None),
        P("head", "seq", None),
        P("head", "seq"),
        P("seq"),
        P("seq"),
        P("head", None, None),
        P("head", None, None),
        P("head", None, None),
        P("head", None),
    )
    return jax.shard_map(
        layer,
        mesh=mesh,
        in_specs=placed,
        out_specs=(P("head", "seq", None), P("seq", "head", None)),
        check_vma=False,
    )
```

```python
import functools
import math
import jax
import jax.numpy as jnp
from jax import lax
from jax.experimental import pallas as pl
from jax.experimental.pallas import tpu as pltpu
from jax.sharding import PartitionSpec as P


F32 = jnp.float32
GRADS_STEP = 256
APPLY_STEP = 256
RENORM_VMEM = 51200 << 10
RELAY_VMEM = 53000 << 10
APPLY_VMEM = 50800 << 10
BF16 = jnp.bfloat16
NN = (((1,), (0,)), ((), ()))
NT = (((1,), (1,)), ((), ()))


def dot(a, b, dims):
    return lax.dot_general(a, b, dims, preferred_element_type=F32)


def grads_kernel(
    k_hbm, v_hbm, wg_hbm, wu_hbm, wd_hbm, rate_ref, flag_ref, out_hbm,
    k_s, v_s, wg_s, wu_s, wd_s, out_s, sem_in, sem_out,
):
    loads = [
        pltpu.make_async_copy(src.at[0], dst, sem_in.at[i])
        for i, (src, dst) in enumerate(
            ((v_hbm, v_s), (wd_hbm, wd_s), (k_hbm, k_s), (wg_hbm, wg_s), (wu_hbm, wu_s))
        )
    ]
    for load in loads:
        load.start()
    step = GRADS_STEP
    part = step // 16
    stores = []

    def put(piece, which, start):
        for c in range(4):
            block = piece[:, c * 128 : (c + 1) * 128].reshape(part, 16, 128)
            row = which * 64 + c * 16
            out_s[start // 16 : start // 16 + part, row : row + 16, :] = block

    def ship(low, high, start, rows):
        window = (slice(start // 16, (start + rows) // 16), slice(low, high))
        store = pltpu.make_async_copy(out_s.at[window], out_hbm.at[window], sem_out.at[len(stores)])
        store.start()
        stores.append(store)

    rate = rate_ref[...]
    coeff = flag_ref[...].astype(F32) * rate
    total = jnp.sum(rate, axis=1, keepdims=True)
    high = total.astype(BF16)
    low = (total - high.astype(F32)).astype(BF16)
    row = lax.broadcasted_iota(jnp.int32, (8, 128), 0)
    tail = jnp.where(row == 0, high.astype(F32), jnp.where(row == 1, low.astype(F32), 0.0))
    out_s[:, 192:200, :] = jnp.broadcast_to(tail.astype(BF16)[None], (32, 8, 128))
    loads[0].wait()
    scaled = (coeff * v_s[...].T.astype(F32)).astype(BF16)
    loads[1].wait()
    down = wd_s[...].T
    for load in loads[2:]:
        load.wait()
    key = k_s[...]
    hidden = []
    for start in range(0, 512, step):
        rows = slice(start, start + step)
        gate = dot(wg_s[rows, :], key, NT)
        up = dot(wu_s[rows, :], key, NT)
        back = dot(down[rows], scaled, NN)
        sigma = jax.nn.sigmoid(gate)
        active = gate * sigma
        hidden.append((active * up).astype(BF16))
        grad_gate = (back * up * sigma * (1.0 + gate * (1.0 - sigma))).astype(BF16)
        grad_up = (back * active).astype(BF16)
        put(dot(grad_gate, key, NN).astype(BF16), 0, start)
        put(dot(grad_up, key, NN).astype(BF16), 1, start)
        ship(0, 128, start, step)
    hidden = jnp.concatenate(hidden, axis=0)
    for start in range(0, 512, step):
        rows = slice(start, start + step)
        put(dot(scaled[rows], hidden, NT).astype(BF16), 2, start)
        ship(128, 200, start, step)
    for store in stores:
        store.wait()


def grads(k, v, rate, flag, wg, wu, wd):
    vm = pl.BlockSpec(memory_space=pltpu.VMEM)
    hb = pl.BlockSpec(memory_space=pltpu.HBM)
    return pl.pallas_call(
        grads_kernel,
        out_shape=jax.ShapeDtypeStruct((32, 200, 128), BF16),
        in_specs=[hb] * 5 + [vm, vm],
        out_specs=hb,
        scratch_shapes=[pltpu.VMEM((512, 512), BF16)] * 5
        + [
            pltpu.VMEM((32, 200, 128), BF16),
            pltpu.SemaphoreType.DMA((5,)),
            pltpu.SemaphoreType.DMA((2 * (512 // GRADS_STEP),)),
        ],
        name="grads",
    )(k, v, wg, wu, wd, rate, flag)


def renorm_kernel(
    spot_ref, recv_ref, wg, wu, wd, left_hbm, right_hbm,
    old_s, left_s, right_s, sem_in, sem_left, sem_right, *, update_len,
):
    rows = pl.ds(pl.multiple_of(lax.rem(spot_ref[0], 32) * 16, 16), 16)
    loads = [
        pltpu.make_async_copy(ref.at[0, rows], old_s.at[i], sem_in.at[i])
        for i, ref in enumerate((wg, wu, wd))
    ]
    for load in loads:
        load.start()
    tail = jnp.sum(recv_ref[:, 192:200, :].astype(F32), axis=0)
    total = tail[0:1, 0:1] + tail[1:2, 0:1]
    factor = 2.0 * update_len / (total * math.sqrt(update_len * 512))
    for which in range(3):
        pieces = []
        for c in range(4):
            row = which * 64 + c * 16
            pieces.append(jnp.sum(recv_ref[:, row : row + 16, :].astype(F32), axis=0))
        summed = jnp.concatenate(pieces, axis=1)
        loads[which].wait()
        old = old_s[which].astype(F32)
        updated = old + summed * factor
        old_norm = jnp.sqrt(jnp.sum(old * old, axis=-1, keepdims=True))
        new_norm = jnp.sqrt(jnp.sum(updated * updated, axis=-1, keepdims=True) + 1e-6)
        fresh = (updated * (old_norm / new_norm)).astype(BF16)
        left_s[which] = fresh[:, :256]
        right_s[which] = fresh[:, 256:]
    stores = [pltpu.make_async_copy(right_s, right_hbm.at[d], sem_right.at[d]) for d in range(16)]
    stores.append(pltpu.make_async_copy(left_s, left_hbm, sem_left))
    for store in stores:
        store.start()
    for store in stores:
        store.wait()


def renorm(spot, recv, wg, wu, wd, update_len):
    hb = pl.BlockSpec(memory_space=pltpu.HBM)
    return pl.pallas_call(
        functools.partial(renorm_kernel, update_len=update_len),
        out_shape=(
            jax.ShapeDtypeStruct((3, 16, 256), BF16),
            jax.ShapeDtypeStruct((16, 3, 16, 256), BF16),
        ),
        in_specs=[
            pl.BlockSpec(memory_space=pltpu.SMEM),
            pl.BlockSpec(memory_space=pltpu.VMEM),
            hb,
            hb,
            hb,
        ],
        out_specs=(hb, hb),
        scratch_shapes=[
            pltpu.VMEM((3, 16, 512), BF16),
            pltpu.VMEM((3, 16, 256), BF16),
            pltpu.VMEM((3, 16, 256), BF16),
            pltpu.SemaphoreType.DMA((3,)),
            pltpu.SemaphoreType.DMA,
            pltpu.SemaphoreType.DMA((16,)),
        ],
        compiler_params=pltpu.CompilerParams(vmem_limit_bytes=RENORM_VMEM),
        name="renorm",
    )(spot, recv, wg, wu, wd)


def attend_kernel(
    pos_ref, doc_ref, q_hbm, k_hbm, v_hbm, pk_hbm, pv_hbm, out_hbm,
    q_ref, k_ref, v_ref, pk_ref, pv_ref, att_s, sem,
):
    base = pos_ref[0] * 512
    loads = [
        pltpu.make_async_copy(src.at[0], dst, sem.at[i])
        for i, (src, dst) in enumerate(
            (
                (q_hbm, q_ref),
                (k_hbm, k_ref),
                (v_hbm, v_ref),
                (pk_hbm, pk_ref),
                (pv_hbm, pv_ref),
            )
        )
    ]
    for load in loads:
        load.start()

    for load in loads:
        load.wait()
    step = 128
    scale = 1.0 / math.sqrt(512)
    doc = (jnp.broadcast_to(doc_ref[...], (8, 512)) - base).T[:, :1]
    for start in range(0, 512, step):
        rows = slice(start, start + step)
        q = q_ref[rows, :]
        keys = jnp.concatenate([pk_ref[start:, :], k_ref[: start + step, :]], axis=0)
        vals = jnp.concatenate([pv_ref[start:, :], v_ref[: start + step, :]], axis=0)
        width = 512 + step
        s = dot(q, keys, NT) * scale
        at = lax.broadcasted_iota(jnp.int32, (step, width), 0) + start
        to = lax.broadcasted_iota(jnp.int32, (step, width), 1) + (start - 512)
        ok = (to <= at) & (to > at - 512) & (to >= doc[rows])
        s = jnp.where(ok, s, -1e30)
        top = jnp.max(s, axis=-1, keepdims=True)
        e = jnp.exp(s - top)
        prob = (e / jnp.sum(e, axis=-1, keepdims=True)).astype(BF16)
        att_s[rows, :] = dot(prob, vals, NN)
    store = pltpu.make_async_copy(att_s, out_hbm.at[0], sem.at[5])
    store.start()
    store.wait()


def attend(pos, q, k, v, doc, pk, pv):
    vm = pl.BlockSpec(memory_space=pltpu.VMEM)
    hb = pl.BlockSpec(memory_space=pltpu.HBM)
    return pl.pallas_call(
        attend_kernel,
        out_shape=jax.ShapeDtypeStruct((2, 512, 512), F32),
        in_specs=[pl.BlockSpec(memory_space=pltpu.SMEM), vm] + [hb] * 5,
        out_specs=hb,
        scratch_shapes=[pltpu.VMEM((512, 512), BF16)] * 5
        + [
            pltpu.VMEM((512, 512), F32),
            pltpu.SemaphoreType.DMA((6,)),
        ],
        name="attend",
    )(pos, doc, q, k, v, pk, pv)


def relay_kernel(
    spot_ref, right, zero, one, two, three, wg, wu, wd, left_hbm, right_hbm,
    left_s, right_s, sem_in, sem_out, sem_right,
):
    first = spot_ref[0] < 32
    layer_z = lax.rem(lax.div(spot_ref[0], 8), 4)
    column = lax.rem(spot_ref[0], 8)

    def send(source):
        store = pltpu.make_async_copy(source, right_hbm, sem_right)
        store.start()
        copies = [pltpu.make_async_copy(left_s, left_hbm.at[d], sem_out.at[d]) for d in range(8)]
        for copy in copies:
            copy.start()
        for copy in copies:
            copy.wait()
        store.wait()

    @pl.when(first)
    def _():
        copies = []
        for i, ref in enumerate((wg, wu, wd)):
            copies.append(
                pltpu.make_async_copy(ref.at[:, column, :, pl.ds(0, 256)], left_s.at[:, i], sem_in.at[i])
            )
            copies.append(
                pltpu.make_async_copy(
                    ref.at[layer_z, :, :, pl.ds(256, 256)], right_s.at[:, i], sem_in.at[i + 3]
                )
            )
        for copy in copies:
            copy.start()
        for copy in copies:
            copy.wait()
        send(right_s)

    @pl.when(jnp.logical_not(first))
    def _():
        copies = [
            pltpu.make_async_copy(src, left_s.at[lax.rem(layer_z + 4 - d, 4)], sem_in.at[d])
            for d, src in enumerate((zero, one, two, three))
        ]
        for copy in copies:
            copy.start()
        for copy in copies:
            copy.wait()
        send(right.at[pl.ds(0, 8)])


def relay(spot, right, lefts, wg, wu, wd):
    sm = pl.BlockSpec(memory_space=pltpu.SMEM)
    vm = pl.BlockSpec(memory_space=pltpu.VMEM)
    hb = pl.BlockSpec(memory_space=pltpu.HBM)
    return pl.pallas_call(
        relay_kernel,
        out_shape=(
            jax.ShapeDtypeStruct((8, 4, 3, 16, 256), BF16),
            jax.ShapeDtypeStruct((8, 3, 16, 256), BF16),
        ),
        in_specs=[sm, vm] + [hb] * 7,
        out_specs=(hb, hb),
        scratch_shapes=[
            pltpu.VMEM((4, 3, 16, 256), BF16),
            pltpu.VMEM((8, 3, 16, 256), BF16),
            pltpu.SemaphoreType.DMA((6,)),
            pltpu.SemaphoreType.DMA((8,)),
            pltpu.SemaphoreType.DMA,
        ],
        compiler_params=pltpu.CompilerParams(vmem_limit_bytes=RELAY_VMEM),
        name="relay",
    )(spot, right, *lefts, *(x.reshape(4, 8, 16, 512) for x in (wg, wu, wd)))


def apply_kernel(
    spot_ref, left, own, one, two, three, q_hbm, att_hbm, wc_hbm, mixed_hbm, part_hbm,
    right, q_s, att_s, wc_s, mixed_s, part_s, sem_in, sem_right, sem_out,
):
    layer_z = lax.rem(lax.div(spot_ref[0], 8), 4)
    slabs = [
        pltpu.make_async_copy(src, right.at[lax.rem(layer_z + 4 - d, 4)], sem_right.at[d])
        for d, src in enumerate((own, one, two, three))
    ]
    for slab in slabs:
        slab.start()
    loads = [
        pltpu.make_async_copy(src, dst, sem_in.at[i])
        for i, (src, dst) in enumerate(((q_hbm.at[0], q_s), (att_hbm.at[0], att_s), (wc_hbm, wc_s)))
    ]
    for load in loads:
        load.start()

    def weight(i, low, count):
        spots = [(z, y) for z in range(low // 128, (low + count) // 128) for y in range(8)]
        return jnp.concatenate(
            [
                jnp.concatenate([left[y, z, i] for z, y in spots], axis=0),
                jnp.concatenate([right[z, y, i] for z, y in spots], axis=0),
            ],
            axis=1,
        )

    step = APPLY_STEP
    loads[0].wait()
    for slab in slabs:
        slab.wait()
    q = q_s[...]
    hidden = []
    for start in range(0, 512, step):
        gate = dot(q, weight(0, start, step), NT)
        up = dot(q, weight(1, start, step), NT)
        hidden.append((gate * jax.nn.sigmoid(gate) * up).astype(BF16))
    hidden = jnp.concatenate(hidden, axis=1)
    loads[1].wait()
    for start in range(0, 512, step):
        cols = slice(start, start + step)
        mixed_s[:, cols] = (att_s[:, cols] + dot(hidden, weight(2, start, step), NT)).astype(BF16)
    stores = [pltpu.make_async_copy(mixed_s, mixed_hbm.at[0], sem_out.at[0])]
    stores[0].start()
    loads[2].wait()
    mixed = mixed_s[...]
    for start in range(0, 512, step):
        cols = slice(start, start + step)
        part_s[:, cols] = dot(mixed, wc_s[:, cols], NN).astype(BF16)
    stores.append(pltpu.make_async_copy(part_s, part_hbm, sem_out.at[1]))
    stores[1].start()
    for store in stores:
        store.wait()


def fast_apply(spot, left, rights, q, att, wc):
    vm = pl.BlockSpec(memory_space=pltpu.VMEM)
    hb = pl.BlockSpec(memory_space=pltpu.HBM)
    return pl.pallas_call(
        apply_kernel,
        out_shape=(
            jax.ShapeDtypeStruct((1, 512, 512), BF16),
            jax.ShapeDtypeStruct((512, 512), BF16),
        ),
        in_specs=[pl.BlockSpec(memory_space=pltpu.SMEM), vm] + [hb] * 7,
        out_specs=(hb, hb),
        scratch_shapes=[
            pltpu.VMEM((4, 8, 3, 16, 256), BF16),
            pltpu.VMEM((512, 512), BF16),
            pltpu.VMEM((512, 512), F32),
            pltpu.VMEM((512, 512), BF16),
            pltpu.VMEM((512, 512), BF16),
            pltpu.VMEM((512, 512), BF16),
            pltpu.SemaphoreType.DMA((3,)),
            pltpu.SemaphoreType.DMA((4,)),
            pltpu.SemaphoreType.DMA((2,)),
        ],
        compiler_params=pltpu.CompilerParams(vmem_limit_bytes=APPLY_VMEM),
        name="fast_apply",
    )(spot, left, *rights, q, att, wc)


def combine_kernel(recv_ref, flag_ref, out_ref):
    summed = jnp.sum(recv_ref[...].astype(F32), axis=0)
    flag = jnp.broadcast_to(flag_ref[...].astype(F32), (8, 64)).T[:, :1]
    out_ref[0] = (summed * flag).astype(BF16)


def combine(recv, flag):
    vm = pl.BlockSpec(memory_space=pltpu.VMEM)
    return pl.pallas_call(
        combine_kernel,
        out_shape=jax.ShapeDtypeStruct((1, 64, 512), BF16),
        in_specs=[vm, vm],
        out_specs=vm,
        compiler_params=pltpu.CompilerParams(vmem_limit_bytes=4 << 20),
        name="combine",
    )(recv, flag)


def layer(q, k, v, rate, doc_start, flag, wg, wu, wd, wc):
    seq_count = lax.axis_size("seq")
    half = seq_count // 2
    index = lax.axis_index("seq").astype(jnp.int32)
    place = lambda z, y: z * 8 + y
    slabs = [[place(z + lift, y) for lift in (0, 4) for y in range(8)] for z in range(4)]
    rows = [[place(z, y) for y in range(8)] for z in range(8)]
    halves = [list(range(half)), list(range(half, seq_count))]
    route = [(i - 1, i) for i in range(1, seq_count)]

    def turn(block, d):
        pairs = [
            (place(z + lift, y), place((z + d) % 4 + lift, y))
            for lift in (0, 4)
            for z in range(4)
            for y in range(8)
        ]
        return lax.ppermute(block, "seq", pairs)

    def lift_up(block, d):
        pairs = [(place(z, y), place((z + d) % 4 + 4, y)) for z in range(4) for y in range(8)]
        return lax.ppermute(block, "seq", pairs)

    spot = index[None]
    terms = grads(k, v, rate, flag[None], wg, wu, wd)
    recv = lax.all_to_all(terms, "seq", 0, 0, axis_index_groups=halves)
    pk = lax.ppermute(k, "seq", route)
    left, right = renorm(spot, recv, wg, wu, wd, 512 * half)
    right = lax.all_to_all(right, "seq", 0, 0, axis_index_groups=slabs)
    lefts = [lift_up(left, d) for d in range(4)]
    pv = lax.ppermute(v, "seq", route)
    left, right = relay(spot, right, lefts, wg, wu, wd)
    left = lax.all_to_all(left, "seq", 0, 0, axis_index_groups=rows)
    rights = [right] + [turn(right, d) for d in range(1, 4)]
    att = attend(spot, q, k, v, doc_start[None], pk, pv)
    mixed, part = fast_apply(spot, left, rights, q, att, wc)
    flags = lax.dynamic_slice_in_dim(flag, lax.axis_index("head") * 64, 64, 0)[None]
    got = lax.all_to_all(part.reshape(8, 64, 512), "head", 0, 0)
    return mixed, combine(got, flags)


def solution(mesh):
    placed = (
        P("head", "seq", None),
        P("head", "seq", None),
        P("head", "seq", None),
        P("head", "seq"),
        P("seq"),
        P("seq"),
        P("head", None, None),
        P("head", None, None),
        P("head", None, None),
        P("head", None),
    )
    return jax.shard_map(
        layer,
        mesh=mesh,
        in_specs=placed,
        out_specs=(P("head", "seq", None), P("seq", "head", None)),
        check_vma=False,
    )
```

```python
import functools
import math
import jax
import jax.numpy as jnp
from jax import lax
from jax.experimental import pallas as pl
from jax.experimental.pallas import tpu as pltpu
from jax.sharding import PartitionSpec as P


F32 = jnp.float32
GRADS_STEP = 256
APPLY_STEP = 256
RENORM_VMEM = 51200 << 10
RELAY_VMEM = 53000 << 10
APPLY_VMEM = 50800 << 10
BF16 = jnp.bfloat16
NN = (((1,), (0,)), ((), ()))
NT = (((1,), (1,)), ((), ()))


def dot(a, b, dims):
    return lax.dot_general(a, b, dims, preferred_element_type=F32)


def grads_kernel(
    k_hbm, v_hbm, wg_hbm, wu_hbm, wd_hbm, rate_ref, flag_ref, out_hbm,
    k_s, v_s, wg_s, wu_s, wd_s, out_s, sem_in, sem_out,
):
    loads = [
        pltpu.make_async_copy(src.at[0], dst, sem_in.at[i])
        for i, (src, dst) in enumerate(
            ((v_hbm, v_s), (wd_hbm, wd_s), (k_hbm, k_s), (wg_hbm, wg_s), (wu_hbm, wu_s))
        )
    ]
    for load in loads:
        load.start()
    step = GRADS_STEP
    part = step // 16
    stores = []

    def put(piece, which, start):
        for c in range(4):
            block = piece[:, c * 128 : (c + 1) * 128].reshape(part, 16, 128)
            row = which * 64 + c * 16
            out_s[start // 16 : start // 16 + part, row : row + 16, :] = block

    def ship(low, high, start, rows):
        window = (slice(start // 16, (start + rows) // 16), slice(low, high))
        store = pltpu.make_async_copy(out_s.at[window], out_hbm.at[window], sem_out.at[len(stores)])
        store.start()
        stores.append(store)

    rate = rate_ref[...]
    coeff = flag_ref[...].astype(F32) * rate
    total = jnp.sum(rate, axis=1, keepdims=True)
    high = total.astype(BF16)
    low = (total - high.astype(F32)).astype(BF16)
    row = lax.broadcasted_iota(jnp.int32, (8, 128), 0)
    tail = jnp.where(row == 0, high.astype(F32), jnp.where(row == 1, low.astype(F32), 0.0))
    out_s[:, 192:200, :] = jnp.broadcast_to(tail.astype(BF16)[None], (32, 8, 128))
    loads[0].wait()
    scaled = (coeff * v_s[...].T.astype(F32)).astype(BF16)
    loads[1].wait()
    down = wd_s[...].T
    for load in loads[2:]:
        load.wait()
    key = k_s[...]
    hidden = []
    for start in range(0, 512, step):
        rows = slice(start, start + step)
        gate = dot(wg_s[rows, :], key, NT)
        up = dot(wu_s[rows, :], key, NT)
        back = dot(down[rows], scaled, NN)
        sigma = jax.nn.sigmoid(gate)
        active = gate * sigma
        hidden.append((active * up).astype(BF16))
        grad_gate = (back * up * sigma * (1.0 + gate * (1.0 - sigma))).astype(BF16)
        grad_up = (back * active).astype(BF16)
        put(dot(grad_gate, key, NN).astype(BF16), 0, start)
        put(dot(grad_up, key, NN).astype(BF16), 1, start)
        ship(0, 128, start, step)
    hidden = jnp.concatenate(hidden, axis=0)
    for start in range(0, 512, step):
        rows = slice(start, start + step)
        put(dot(scaled[rows], hidden, NT).astype(BF16), 2, start)
        ship(128, 200, start, step)
    for store in stores:
        store.wait()


def grads(k, v, rate, flag, wg, wu, wd):
    vm = pl.BlockSpec(memory_space=pltpu.VMEM)
    hb = pl.BlockSpec(memory_space=pltpu.HBM)
    return pl.pallas_call(
        grads_kernel,
        out_shape=jax.ShapeDtypeStruct((32, 200, 128), BF16),
        in_specs=[hb] * 5 + [vm, vm],
        out_specs=hb,
        scratch_shapes=[pltpu.VMEM((512, 512), BF16)] * 5
        + [
            pltpu.VMEM((32, 200, 128), BF16),
            pltpu.SemaphoreType.DMA((5,)),
            pltpu.SemaphoreType.DMA((2 * (512 // GRADS_STEP),)),
        ],
        name="grads",
    )(k, v, wg, wu, wd, rate, flag)


def renorm_kernel(
    spot_ref, recv_ref, wg, wu, wd, left_hbm, right_hbm,
    old_s, left_s, right_s, sem_in, sem_left, sem_right, *, update_len,
):
    rows = pl.ds(pl.multiple_of(lax.rem(spot_ref[0], 32) * 16, 16), 16)
    loads = [
        pltpu.make_async_copy(ref.at[0, rows], old_s.at[i], sem_in.at[i])
        for i, ref in enumerate((wg, wu, wd))
    ]
    for load in loads:
        load.start()
    tail = jnp.sum(recv_ref[:, 192:200, :].astype(F32), axis=0)
    total = tail[0:1, 0:1] + tail[1:2, 0:1]
    factor = 2.0 * update_len / (total * math.sqrt(update_len * 512))
    for which in range(3):
        pieces = []
        for c in range(4):
            row = which * 64 + c * 16
            pieces.append(jnp.sum(recv_ref[:, row : row + 16, :].astype(F32), axis=0))
        summed = jnp.concatenate(pieces, axis=1)
        loads[which].wait()
        old = old_s[which].astype(F32)
        updated = old + summed * factor
        old_norm = jnp.sqrt(jnp.sum(old * old, axis=-1, keepdims=True))
        new_norm = jnp.sqrt(jnp.sum(updated * updated, axis=-1, keepdims=True) + 1e-6)
        fresh = (updated * (old_norm / new_norm)).astype(BF16)
        left_s[which] = fresh[:, :256]
        right_s[which] = fresh[:, 256:]
    stores = [pltpu.make_async_copy(right_s, right_hbm.at[d], sem_right.at[d]) for d in range(16)]
    stores.append(pltpu.make_async_copy(left_s, left_hbm, sem_left))
    for store in stores:
        store.start()
    for store in stores:
        store.wait()


def renorm(spot, recv, wg, wu, wd, update_len):
    hb = pl.BlockSpec(memory_space=pltpu.HBM)
    return pl.pallas_call(
        functools.partial(renorm_kernel, update_len=update_len),
        out_shape=(
            jax.ShapeDtypeStruct((3, 16, 256), BF16),
            jax.ShapeDtypeStruct((16, 3, 16, 256), BF16),
        ),
        in_specs=[
            pl.BlockSpec(memory_space=pltpu.SMEM),
            pl.BlockSpec(memory_space=pltpu.VMEM),
            hb,
            hb,
            hb,
        ],
        out_specs=(hb, hb),
        scratch_shapes=[
            pltpu.VMEM((3, 16, 512), BF16),
            pltpu.VMEM((3, 16, 256), BF16),
            pltpu.VMEM((3, 16, 256), BF16),
            pltpu.SemaphoreType.DMA((3,)),
            pltpu.SemaphoreType.DMA,
            pltpu.SemaphoreType.DMA((16,)),
        ],
        compiler_params=pltpu.CompilerParams(vmem_limit_bytes=RENORM_VMEM),
        name="renorm",
    )(spot, recv, wg, wu, wd)


def attend_kernel(
    pos_ref, doc_ref, q_hbm, k_hbm, v_hbm, pk_hbm, pv_hbm, edge_k, edge_v, out_hbm,
    q_ref, k_ref, v_ref, pk_ref, pv_ref, att_s, sem,
):
    base = pos_ref[0] * 512
    loads = [
        pltpu.make_async_copy(src.at[0], dst, sem.at[i])
        for i, (src, dst) in enumerate(((q_hbm, q_ref), (k_hbm, k_ref), (v_hbm, v_ref)))
    ]
    for load in loads:
        load.start()

    def fetch(src_k, src_v):
        return (
            pltpu.make_async_copy(src_k.at[0], pk_ref, sem.at[3]),
            pltpu.make_async_copy(src_v.at[0], pv_ref, sem.at[4]),
        )

    at_edge = lax.rem(pos_ref[0], 8) == 0

    @pl.when(at_edge)
    def _():
        for copy in fetch(edge_k, edge_v):
            copy.start()

    @pl.when(jnp.logical_not(at_edge))
    def _():
        for copy in fetch(pk_hbm, pv_hbm):
            copy.start()

    loads += fetch(pk_hbm, pv_hbm)
    for load in loads:
        load.wait()
    step = 128
    scale = 1.0 / math.sqrt(512)
    doc = (jnp.broadcast_to(doc_ref[...], (8, 512)) - base).T[:, :1]
    for start in range(0, 512, step):
        rows = slice(start, start + step)
        q = q_ref[rows, :]
        keys = jnp.concatenate([pk_ref[start:, :], k_ref[: start + step, :]], axis=0)
        vals = jnp.concatenate([pv_ref[start:, :], v_ref[: start + step, :]], axis=0)
        width = 512 + step
        s = dot(q, keys, NT) * scale
        at = lax.broadcasted_iota(jnp.int32, (step, width), 0) + start
        to = lax.broadcasted_iota(jnp.int32, (step, width), 1) + (start - 512)
        ok = (to <= at) & (to > at - 512) & (to >= doc[rows])
        s = jnp.where(ok, s, -1e30)
        top = jnp.max(s, axis=-1, keepdims=True)
        e = jnp.exp(s - top)
        prob = (e / jnp.sum(e, axis=-1, keepdims=True)).astype(BF16)
        att_s[rows, :] = dot(prob, vals, NN)
    store = pltpu.make_async_copy(att_s, out_hbm.at[0], sem.at[5])
    store.start()
    store.wait()


def attend(pos, q, k, v, doc, pk, pv, edge_k, edge_v):
    vm = pl.BlockSpec(memory_space=pltpu.VMEM)
    hb = pl.BlockSpec(memory_space=pltpu.HBM)
    return pl.pallas_call(
        attend_kernel,
        out_shape=jax.ShapeDtypeStruct((2, 512, 512), F32),
        in_specs=[pl.BlockSpec(memory_space=pltpu.SMEM), vm] + [hb] * 7,
        out_specs=hb,
        scratch_shapes=[pltpu.VMEM((512, 512), BF16)] * 5
        + [
            pltpu.VMEM((512, 512), F32),
            pltpu.SemaphoreType.DMA((6,)),
        ],
        name="attend",
    )(pos, doc, q, k, v, pk, pv, edge_k, edge_v)


def relay_kernel(
    spot_ref, right, zero, one, two, three, wg, wu, wd, left_hbm, right_hbm,
    left_s, right_s, sem_in, sem_out, sem_right,
):
    first = spot_ref[0] < 32
    layer_z = lax.rem(lax.div(spot_ref[0], 8), 4)
    column = lax.rem(spot_ref[0], 8)

    def send(source):
        store = pltpu.make_async_copy(source, right_hbm, sem_right)
        store.start()
        copies = [pltpu.make_async_copy(left_s, left_hbm.at[d], sem_out.at[d]) for d in range(8)]
        for copy in copies:
            copy.start()
        for copy in copies:
            copy.wait()
        store.wait()

    @pl.when(first)
    def _():
        copies = []
        for i, ref in enumerate((wg, wu, wd)):
            copies.append(
                pltpu.make_async_copy(ref.at[:, column, :, pl.ds(0, 256)], left_s.at[:, i], sem_in.at[i])
            )
            copies.append(
                pltpu.make_async_copy(
                    ref.at[layer_z, :, :, pl.ds(256, 256)], right_s.at[:, i], sem_in.at[i + 3]
                )
            )
        for copy in copies:
            copy.start()
        for copy in copies:
            copy.wait()
        send(right_s)

    @pl.when(jnp.logical_not(first))
    def _():
        copies = [
            pltpu.make_async_copy(src, left_s.at[lax.rem(layer_z + 4 - d, 4)], sem_in.at[d])
            for d, src in enumerate((zero, one, two, three))
        ]
        for copy in copies:
            copy.start()
        for copy in copies:
            copy.wait()
        send(right.at[pl.ds(0, 8)])


def relay(spot, right, lefts, wg, wu, wd):
    sm = pl.BlockSpec(memory_space=pltpu.SMEM)
    vm = pl.BlockSpec(memory_space=pltpu.VMEM)
    hb = pl.BlockSpec(memory_space=pltpu.HBM)
    return pl.pallas_call(
        relay_kernel,
        out_shape=(
            jax.ShapeDtypeStruct((8, 4, 3, 16, 256), BF16),
            jax.ShapeDtypeStruct((8, 3, 16, 256), BF16),
        ),
        in_specs=[sm, vm] + [hb] * 7,
        out_specs=(hb, hb),
        scratch_shapes=[
            pltpu.VMEM((4, 3, 16, 256), BF16),
            pltpu.VMEM((8, 3, 16, 256), BF16),
            pltpu.SemaphoreType.DMA((6,)),
            pltpu.SemaphoreType.DMA((8,)),
            pltpu.SemaphoreType.DMA,
        ],
        compiler_params=pltpu.CompilerParams(vmem_limit_bytes=RELAY_VMEM),
        name="relay",
    )(spot, right, *lefts, *(x.reshape(4, 8, 16, 512) for x in (wg, wu, wd)))


def apply_kernel(
    spot_ref, left, own, one, two, three, q_hbm, att_hbm, wc_hbm, mixed_hbm, part_hbm,
    right, q_s, att_s, wc_s, mixed_s, part_s, sem_in, sem_right, sem_out,
):
    layer_z = lax.rem(lax.div(spot_ref[0], 8), 4)
    slabs = [
        pltpu.make_async_copy(src, right.at[lax.rem(layer_z + 4 - d, 4)], sem_right.at[d])
        for d, src in enumerate((own, one, two, three))
    ]
    for slab in slabs:
        slab.start()
    loads = [
        pltpu.make_async_copy(src, dst, sem_in.at[i])
        for i, (src, dst) in enumerate(((q_hbm.at[0], q_s), (att_hbm.at[0], att_s), (wc_hbm, wc_s)))
    ]
    for load in loads:
        load.start()

    def weight(i, low, count):
        spots = [(z, y) for z in range(low // 128, (low + count) // 128) for y in range(8)]
        return jnp.concatenate(
            [
                jnp.concatenate([left[y, z, i] for z, y in spots], axis=0),
                jnp.concatenate([right[z, y, i] for z, y in spots], axis=0),
            ],
            axis=1,
        )

    step = APPLY_STEP
    loads[0].wait()
    for slab in slabs:
        slab.wait()
    q = q_s[...]
    hidden = []
    for start in range(0, 512, step):
        gate = dot(q, weight(0, start, step), NT)
        up = dot(q, weight(1, start, step), NT)
        hidden.append((gate * jax.nn.sigmoid(gate) * up).astype(BF16))
    hidden = jnp.concatenate(hidden, axis=1)
    loads[1].wait()
    for start in range(0, 512, step):
        cols = slice(start, start + step)
        mixed_s[:, cols] = (att_s[:, cols] + dot(hidden, weight(2, start, step), NT)).astype(BF16)
    stores = [pltpu.make_async_copy(mixed_s, mixed_hbm.at[0], sem_out.at[0])]
    stores[0].start()
    loads[2].wait()
    mixed = mixed_s[...]
    for start in range(0, 512, step):
        cols = slice(start, start + step)
        part_s[:, cols] = dot(mixed, wc_s[:, cols], NN).astype(BF16)
    stores.append(pltpu.make_async_copy(part_s, part_hbm, sem_out.at[1]))
    stores[1].start()
    for store in stores:
        store.wait()


def fast_apply(spot, left, rights, q, att, wc):
    vm = pl.BlockSpec(memory_space=pltpu.VMEM)
    hb = pl.BlockSpec(memory_space=pltpu.HBM)
    return pl.pallas_call(
        apply_kernel,
        out_shape=(
            jax.ShapeDtypeStruct((1, 512, 512), BF16),
            jax.ShapeDtypeStruct((512, 512), BF16),
        ),
        in_specs=[pl.BlockSpec(memory_space=pltpu.SMEM), vm] + [hb] * 7,
        out_specs=(hb, hb),
        scratch_shapes=[
            pltpu.VMEM((4, 8, 3, 16, 256), BF16),
            pltpu.VMEM((512, 512), BF16),
            pltpu.VMEM((512, 512), F32),
            pltpu.VMEM((512, 512), BF16),
            pltpu.VMEM((512, 512), BF16),
            pltpu.VMEM((512, 512), BF16),
            pltpu.SemaphoreType.DMA((3,)),
            pltpu.SemaphoreType.DMA((4,)),
            pltpu.SemaphoreType.DMA((2,)),
        ],
        compiler_params=pltpu.CompilerParams(vmem_limit_bytes=APPLY_VMEM),
        name="fast_apply",
    )(spot, left, *rights, q, att, wc)


def combine_kernel(recv_ref, flag_ref, out_ref):
    summed = jnp.sum(recv_ref[...].astype(F32), axis=0)
    flag = jnp.broadcast_to(flag_ref[...].astype(F32), (8, 64)).T[:, :1]
    out_ref[0] = (summed * flag).astype(BF16)


def combine(recv, flag):
    vm = pl.BlockSpec(memory_space=pltpu.VMEM)
    return pl.pallas_call(
        combine_kernel,
        out_shape=jax.ShapeDtypeStruct((1, 64, 512), BF16),
        in_specs=[vm, vm],
        out_specs=vm,
        compiler_params=pltpu.CompilerParams(vmem_limit_bytes=4 << 20),
        name="combine",
    )(recv, flag)


def layer(q, k, v, rate, doc_start, flag, wg, wu, wd, wc):
    seq_count = lax.axis_size("seq")
    half = seq_count // 2
    index = lax.axis_index("seq").astype(jnp.int32)
    place = lambda z, y: z * 8 + y
    slabs = [[place(z + lift, y) for lift in (0, 4) for y in range(8)] for z in range(4)]
    rows = [[place(z, y) for y in range(8)] for z in range(8)]
    halves = [list(range(half)), list(range(half, seq_count))]
    edge = [(i - 1, i) for i in range(8, seq_count, 8)]
    route = [(i - 1, i) for i in range(1, seq_count) if i % 8]

    def turn(block, d):
        pairs = [
            (place(z + lift, y), place((z + d) % 4 + lift, y))
            for lift in (0, 4)
            for z in range(4)
            for y in range(8)
        ]
        return lax.ppermute(block, "seq", pairs)

    def lift_up(block, d):
        pairs = [(place(z, y), place((z + d) % 4 + 4, y)) for z in range(4) for y in range(8)]
        return lax.ppermute(block, "seq", pairs)

    spot = index[None]
    edge_k = lax.ppermute(k, "seq", edge)
    edge_v = lax.ppermute(v, "seq", edge)
    terms = grads(k, v, rate, flag[None], wg, wu, wd)
    recv = lax.all_to_all(terms, "seq", 0, 0, axis_index_groups=halves)
    pk = lax.ppermute(k, "seq", route)
    left, right = renorm(spot, recv, wg, wu, wd, 512 * half)
    right = lax.all_to_all(right, "seq", 0, 0, axis_index_groups=slabs)
    lefts = [lift_up(left, d) for d in range(4)]
    pv = lax.ppermute(v, "seq", route)
    left, right = relay(spot, right, lefts, wg, wu, wd)
    left = lax.all_to_all(left, "seq", 0, 0, axis_index_groups=rows)
    rights = [right] + [turn(right, d) for d in range(1, 4)]
    att = attend(spot, q, k, v, doc_start[None], pk, pv, edge_k, edge_v)
    mixed, part = fast_apply(spot, left, rights, q, att, wc)
    flags = lax.dynamic_slice_in_dim(flag, lax.axis_index("head") * 64, 64, 0)[None]
    got = lax.all_to_all(part.reshape(8, 64, 512), "head", 0, 0)
    return mixed, combine(got, flags)


def solution(mesh):
    placed = (
        P("head", "seq", None),
        P("head", "seq", None),
        P("head", "seq", None),
        P("head", "seq"),
        P("seq"),
        P("seq"),
        P("head", None, None),
        P("head", None, None),
        P("head", None, None),
        P("head", None),
    )
    return jax.shard_map(
        layer,
        mesh=mesh,
        in_specs=placed,
        out_specs=(P("head", "seq", None), P("seq", "head", None)),
        check_vma=False,
    )
```
